512 devices in a mesh: px: 32 (over y, x, core), py: 16 (over z).
Axes of the slice: x: 4, y: 4, z: 16, core: 2. Of those that a mesh axis runs over, the one named last changes fastest.
Arguments:
- currents_in: bfloat16 [64, 32, 2, 32, 512], P('px', 'py'), may hold values from -6 to 6
- rad_pattern: bfloat16 [2, 512, 512], replicated, may hold values from -0.1875 to 0.1875
- far_map: bfloat16 [512, 2048], replicated, may hold values from -0.25 to 0.25
- reflect: float32 [64, 32, 512], P('px', 'py'), may hold values from 0.2 to 0.7
- centres: float32 [3, 64, 32], P(None, 'px', 'py'), may hold values from -30 to 30
- spectral_dirs: float32 [3, 512], replicated, may hold values from -3 to 3
- receiver_dirs: float32 [3, 2048], replicated, may hold values from -3 to 3
- partners: int32 [64, 32, 12], P('px', 'py'), may hold values from 0 to 2047, as said below
- partner_count: int32 [64, 32], P('px', 'py'), may hold values from 1 to 12, as said below
- pair_weight: bfloat16 [64, 32, 12], P('px', 'py'), may hold values from 0.29882812 to 1
Outputs:
- currents: bfloat16 [64, 32, 2, 32, 512], P('px', 'py')
- isar_image: float32 [32, 2048], P('py', 'px')
The draws below stay inside these ranges and needn't reach their ends.
Inputs may be any that keep to these rules, and one draw needn't show every extreme that they name: `partners`: the first partner_count entries of a patch's list are distinct patches other than itself, at most 1 patch rows away along the hull and, counting columns around the girth (column indices wrap modulo 32), at most 2 columns away; later entries are valid patch ids that are ignored. `partner_count`: some patch lists 12 partners.
All inputs are finite; a program needn't handle non-finite values.
Results may differ from the reference program's by a relative error of at most 0.019.
Values may be sent and summed in bfloat16 or wider, within the bound.
A program may use at most 64 MiB of HBM per device.

```python
import math
import jax
import jax.numpy as jnp
from jax import lax

PR = 2
PC = 2
K = 32
B = 512
M = 512
R = 2048
SLOTS = 12
ROW_REACH = 1
COL_REACH = 2
NR = 64
NC = 32


def visibility(key):
    base = jax.random.fold_in(key, 4242)
    k_pick, k_band, k_low, k_high, k_row, k_col = jax.random.split(base, 6)
    offsets = [(a, b) for a in range(-ROW_REACH, ROW_REACH + 1) for b in range(-COL_REACH, COL_REACH + 1) if (a, b) != (0, 0)]
    row_shift = jnp.array([o[0] for o in offsets], jnp.int32)
    col_shift = jnp.array([o[1] for o in offsets], jnp.int32)
    n_offsets = len(offsets)
    row_ids = jnp.arange(NR, dtype=jnp.int32)[:, None, None]
    col_ids = jnp.arange(NC, dtype=jnp.int32)[None, :, None]
    target_row = row_ids + row_shift[None, None, :]
    usable = (target_row >= 0) & (target_row < NR)
    usable = jnp.broadcast_to(usable, (NR, NC, n_offsets))
    score = jax.random.randint(k_pick, (NR, NC, n_offsets), 0, 1 << 20) * 64 + jnp.arange(n_offsets, dtype=jnp.int32)
    score = jnp.where(usable, score, (1 << 27) + jnp.arange(n_offsets, dtype=jnp.int32))
    order = jnp.argsort(score, axis=-1, stable=True)[..., :SLOTS]
    pick_row = jnp.clip(jnp.take(row_shift, order) + row_ids, 0, NR - 1)
    pick_col = (jnp.take(col_shift, order) + col_ids) % NC
    partner_ids = pick_row * NC + pick_col
    blocks = jax.random.randint(k_band, (NR // PR, NC // PC), 0, 4)
    busy = jnp.repeat(jnp.repeat(blocks, PR, axis=0), PC, axis=1) == 3
    low_count = jax.random.randint(k_low, (NR, NC), 1, 6)
    high_count = jax.random.randint(k_high, (NR, NC), 8, SLOTS + 1)
    wanted = jnp.where(busy, high_count, low_count)
    wanted = jnp.minimum(wanted, jnp.sum(usable.astype(jnp.int32), axis=-1))
    force_row = jax.random.randint(k_row, (), ROW_REACH, NR - ROW_REACH)
    force_col = jax.random.randint(k_col, (), 0, NC)
    hit = (row_ids[:, :, 0] == force_row) & (col_ids[:, :, 0] == force_col)
    counts = jnp.where(hit, SLOTS, wanted)
    return (counts.astype(jnp.int32), partner_ids.astype(jnp.int32))


def draw_partners(key, part):
    return visibility(key)[1]


def draw_partner_count(key, part):
    return visibility(key)[0]


def shard_levels(own_key, extent, cuts, smallest, largest):
    gain = 1.0
    for position, shards_of in cuts:
        draws = jax.random.uniform(jax.random.fold_in(jax.random.fold_in(own_key, 6), position), (shards_of,), jnp.float32, smallest / len(cuts), largest / len(cuts))
        gain = gain * jnp.repeat(jnp.exp(draws), extent[position] // shards_of).reshape((-1,) + (1,) * (len(extent) - 1 - position))
    return gain


def noise(key, dims, width, most, cuts=(), held_as=jnp.bfloat16):
    entries = width * jax.random.normal(key, dims, jnp.float32)
    if cuts:
        entries = entries * shard_levels(key, dims, cuts, -0.22, 0.18)
    return jnp.clip(entries, -most, most).astype(held_as)


def setup_inputs(seed: int = 0) -> dict:
    arg_keys = jax.random.split(jax.random.key(seed), 11)
    currents_in = noise(arg_keys[0], (NR, NC, 2, K, B), 1.0, 6.0, ((0, 32), (1, 16)))
    rad_pattern = noise(arg_keys[1], (2, B, M), (2 * B) ** -0.5, 0.1875)
    far_map = noise(arg_keys[2], (M, R), M ** -0.5, 0.25)
    reflect = jnp.clip(0.2 + 0.5 * jax.random.uniform(arg_keys[3], (NR, NC, B), jnp.float32) ** shard_levels(arg_keys[3], (NR, NC, B), ((0, 32), (1, 16)), -0.2, 0.2), 0.2, 0.7)
    centres = jnp.clip(jax.random.uniform(arg_keys[4], (3, NR, NC), jnp.float32, -30.0, 30.0) * shard_levels(arg_keys[4], (3, NR, NC), ((1, 32), (2, 16)), -0.4, 0.0), -30.0, 30.0)
    spectral_dirs = noise(arg_keys[5], (3, M), 0.6, 3.0, (), jnp.float32)
    receiver_dirs = noise(arg_keys[6], (3, R), 0.6, 3.0, (), jnp.float32)
    partners = draw_partners(jax.random.fold_in(arg_keys[10], 71), 0)
    partner_count = draw_partner_count(jax.random.fold_in(arg_keys[10], 71), 0)
    pair_weight = jnp.clip(0.29882812 + 0.7011719 * jax.random.uniform(arg_keys[9], (NR, NC, SLOTS), jnp.float32) ** shard_levels(arg_keys[9], (NR, NC, SLOTS), ((0, 32), (1, 16)), -0.2, 0.2), 0.29882812, 1.0).astype(jnp.bfloat16)
    return dict(currents_in=currents_in, rad_pattern=rad_pattern, far_map=far_map, reflect=reflect, centres=centres, spectral_dirs=spectral_dirs, receiver_dirs=receiver_dirs, partners=partners, partner_count=partner_count, pair_weight=pair_weight)


def angles(dirs, centres):
    return jnp.einsum('dm,dab->abm', dirs, centres, precision=lax.Precision.HIGHEST)

def matmul(left, right):
    return jnp.dot(left, right, preferred_element_type=jnp.float32)

def radiate(currents, rad_pattern):
    flat_re = currents[:, :, 0].reshape(-1, B)
    flat_im = currents[:, :, 1].reshape(-1, B)
    spec_re = matmul(flat_re, rad_pattern[0]) - matmul(flat_im, rad_pattern[1])
    spec_im = matmul(flat_re, rad_pattern[1]) + matmul(flat_im, rad_pattern[0])
    return (spec_re.reshape(NR, NC, K, M), spec_im.reshape(NR, NC, K, M))

def bounce(current_now, currents_in, rad_pattern, reflect, phi, partners, partner_count, pair_weight):
    spec_re, spec_im = radiate(current_now, rad_pattern)
    cosine = jnp.cos(phi)[:, :, None, :]
    sine_part = jnp.sin(phi)[:, :, None, :]
    out_re = spec_re * cosine + spec_im * sine_part
    out_im = spec_im * cosine - spec_re * sine_part
    outgoing = jnp.stack([out_re, out_im], axis=2).astype(jnp.bfloat16)
    patch_total = NR * NC
    flat_out = outgoing.reshape(patch_total, 2 * K * M)
    list_ids = partners.reshape(patch_total, SLOTS).astype(jnp.int32)
    live = jnp.arange(SLOTS, dtype=jnp.int32)[None, :] < partner_count.reshape(patch_total, 1)
    weights = jnp.where(live, pair_weight.reshape(patch_total, SLOTS).astype(jnp.float32), jnp.float32(0.0))

    def step(running, slot_id):
        picked = jnp.take(flat_out, list_ids[:, slot_id], axis=0).astype(jnp.float32)
        return (running + weights[:, slot_id][:, None] * picked, None)
    start = jnp.zeros((patch_total, 2 * K * M), jnp.float32)
    collected, _ = lax.scan(step, start, jnp.arange(SLOTS, dtype=jnp.int32))
    collected = collected.reshape(NR, NC, 2, K, M)
    col_re, col_im = (collected[:, :, 0], collected[:, :, 1])
    arr_re = (col_re * cosine - col_im * sine_part).astype(jnp.bfloat16).reshape(-1, M)
    arr_im = (col_re * sine_part + col_im * cosine).astype(jnp.bfloat16).reshape(-1, M)
    recv_re = matmul(arr_re, rad_pattern[0].T) - matmul(arr_im, rad_pattern[1].T)
    recv_im = matmul(arr_re, rad_pattern[1].T) + matmul(arr_im, rad_pattern[0].T)
    received = jnp.stack([recv_re.reshape(NR, NC, K, B), recv_im.reshape(NR, NC, K, B)], axis=2)
    updated = currents_in.astype(jnp.float32) + reflect[:, :, None, None, :] * received
    return updated.astype(jnp.bfloat16)

def reference(currents_in, rad_pattern, far_map, reflect, centres, spectral_dirs, receiver_dirs, partners, partner_count, pair_weight):
    phi = angles(spectral_dirs, centres)
    current_now = currents_in
    for bounce_id in range(2):
        current_now = bounce(current_now, currents_in, rad_pattern, reflect, phi, partners, partner_count, pair_weight)
    spec_re, spec_im = radiate(current_now, rad_pattern)
    spec_re = spec_re.astype(jnp.bfloat16)
    spec_im = spec_im.astype(jnp.bfloat16)
    view = angles(receiver_dirs, centres)

    def row_step(running, pieces):
        row_re, row_im, row_view = pieces
        beam_re = matmul(row_re.reshape(-1, M), far_map).reshape(NC, K, R)
        beam_im = matmul(row_im.reshape(-1, M), far_map).reshape(NC, K, R)
        cos_view = jnp.cos(row_view)[:, None, :]
        sin_view = jnp.sin(row_view)[:, None, :]
        far_re = lax.optimization_barrier(jnp.sum(beam_re * cos_view - beam_im * sin_view, axis=0))
        far_im = lax.optimization_barrier(jnp.sum(beam_re * sin_view + beam_im * cos_view, axis=0))
        return ((running[0] + far_re, running[1] + far_im), None)
    start = (jnp.zeros((K, R), jnp.float32), jnp.zeros((K, R), jnp.float32))
    (far_re, far_im), _ = lax.scan(row_step, start, (spec_re, spec_im, view))
    factor = 1.0 / math.sqrt(NR * NC)
    far_re = far_re * factor
    far_im = far_im * factor
    rcv_ids = jnp.arange(R, dtype=jnp.int32)[:, None]
    bin_ids = jnp.arange(R, dtype=jnp.int32)[None, :]
    turn_angle = (rcv_ids * bin_ids % R).astype(jnp.float32) * (2.0 * math.pi / R)
    norm_factor = 1.0 / math.sqrt(R)
    cos_table = jnp.cos(turn_angle) * norm_factor
    sin_table = jnp.sin(turn_angle) * norm_factor
    high = lax.Precision.HIGHEST
    image_re = jnp.dot(far_re, cos_table, precision=high) + jnp.dot(far_im, sin_table, precision=high)
    image_im = jnp.dot(far_im, cos_table, precision=high) - jnp.dot(far_re, sin_table, precision=high)
    isar_image = 0.125 * (image_re * image_re + image_im * image_im)
    return (current_now, isar_image)
```

```python
import math

import numpy as np

import jax
import jax.numpy as jnp
from jax import lax
from jax.experimental import pallas as pl
from jax.experimental.pallas import tpu as pltpu
from jax.sharding import PartitionSpec as P

MESH = pl.DeviceIdType.MESH
F32 = jnp.float32
BF16 = jnp.bfloat16
SLOTS = 12
G = 4
KC = 8
TW = 16
LN = 128


def fft(values):
    size = len(values)
    if size == 1:
        return values
    even = fft(values[0::2])
    odd = fft(values[1::2])
    low, high = [], []
    for t in range(size // 2):
        re, im = odd[t]
        if t == 0:
            pass
        elif 4 * t == size:
            re, im = im, -re
        else:
            c = math.cos(2 * math.pi * t / size)
            s = math.sin(2 * math.pi * t / size)
            if 8 * t == size:
                re, im = (re + im) * c, (im - re) * c
            elif 8 * t == 3 * size:
                re, im = (im - re) * s, (re + im) * (-s)
            else:
                re, im = re * c + im * s, im * c - re * s
        er, ei = even[t]
        low.append((er + re, ei + im))
        high.append((er - re, ei - im))
    return low + high


def doubling(count):
    radii, radius = [], 1
    while 2 * radius <= count // 2:
        radii.append(radius)
        radius *= 2
    return radii


def make_kernel(n_px, n_z, illum, rcv):
    cols_total = 2 * n_z
    patches = 4 * n_px * n_z
    qp = LN // n_px
    rows_p = 2 * qp
    kz = illum // n_z
    hz = KC // kz
    z_rounds = doubling(n_z)
    x_rounds = doubling(n_px)
    scale = 0.125 / (patches * rcv)

    def kernel(
        cin_h, rad_h, far_h, refl_h, cen_h, sd_h, rd_h, part_h, cnt_h, pw_h, fm_h, tw_h,
        cur_h, img_o,
        cin_v, rad_v, radt_v, far_v, refl_v, cen_v, sd_v, rd_v, part_v, cnt_v, pw_v, fm_v, tw_v,
        w_v, wr_v, cs_v, cv_v, cinc_v, x_v, own_v, zr_v, acc_v, push_v, pr_v, curf_v,
        u_v, y_v, sb_v, rb_v, zs_v, zb_v, cur_v,
        in_sem, w_sem, zx_sem, px_sem, rs_sem, zs_sem, out_sem, zd_sem, xd_sem,
    ):
        pi = lax.axis_index("px")
        zi = lax.axis_index("py")

        def ring(value, count):
            return lax.rem(value + count, count)

        z_nb = (ring(zi - 1, n_z), ring(zi + 1, n_z))
        x_nb = (ring(pi - 1, n_px), ring(pi + 1, n_px))

        def z_dev(z):
            return (pi, z)

        def x_dev(x):
            return (x, zi)

        barrier = pltpu.get_barrier_semaphore()
        for z in z_nb:
            pl.semaphore_signal(barrier, inc=1, device_id=z_dev(z), device_id_type=MESH)
        for x in x_nb:
            pl.semaphore_signal(barrier, inc=1, device_id=x_dev(x), device_id_type=MESH)

        ins = []
        for n, (src, dst) in enumerate(
            (
                (cin_h, cin_v), (sd_h, sd_v), (cen_h, cen_v), (rad_h, rad_v),
                (part_h, part_v), (cnt_h, cnt_v), (pw_h, pw_v), (refl_h, refl_v),
                (rd_h, rd_v), (tw_h, tw_v), (fm_h, fm_v), (far_h, far_v),
            )
        ):
            copy = pltpu.make_async_copy(src, dst, in_sem.at[n])
            copy.start()
            ins.append(copy)
        (i_cin, i_sd, i_cen, i_rad, i_part, i_cnt, i_pw, i_refl, i_rd, i_tw, i_fm, i_far) = ins

        def phases(dirs, out):
            for a in range(2):
                for b in range(2):
                    total = None
                    for d in range(3):
                        term = dirs[d : d + 1, :] * cen_v[d, a : a + 1, b : b + 1]
                        total = term if total is None else total + term
                    out[0, 2 * a + b : 2 * a + b + 1, :] = total
            phi = out[0, 0:4, :]
            out[0, 0:4, :] = jnp.cos(phi)
            out[1, 0:4, :] = jnp.sin(phi)

        i_sd.wait()
        i_cen.wait()
        phases(sd_v, cs_v)

        i_cin.wait()
        for p in range(4):
            x0 = cin_v[p // 2, p % 2, 0].astype(F32)
            x1 = cin_v[p // 2, p % 2, 1].astype(F32)
            for g in range(G):
                both = jnp.concatenate([x0[KC * g : KC * g + KC], x1[KC * g : KC * g + KC]], axis=0)
                cinc_v[g, 16 * p : 16 * p + 16, :] = both.astype(BF16)
        i_rad.wait()

        def spectrum(x):
            x0 = jnp.dot(x, rad_v[0], preferred_element_type=F32)
            x1 = jnp.dot(x, rad_v[1], preferred_element_type=F32)
            out = []
            for p in range(4):
                r, i = 16 * p, 16 * p + 8
                out.append((x0[r : r + 8] - x1[i : i + 8], x1[r : r + 8] + x0[i : i + 8]))
            return out

        def z_copy(t, g, d):
            return pltpu.make_async_remote_copy(
                src_ref=own_v.at[t, g],
                dst_ref=zr_v.at[t, g, 1 - d],
                send_sem=zx_sem.at[0, t, g, d],
                recv_sem=zx_sem.at[1, t, g, 1 - d],
                device_id=z_dev(z_nb[d]),
                device_id_type=MESH,
            )

        def x_copy(t, g, d):
            return pltpu.make_async_remote_copy(
                src_ref=push_v.at[t, g, d],
                dst_ref=pr_v.at[t, g, 1 - d],
                send_sem=px_sem.at[0, t, g, d],
                recv_sem=px_sem.at[1, t, g, 1 - d],
                device_id=x_dev(x_nb[d]),
                device_id_type=MESH,
            )

        def w_copy(d):
            return pltpu.make_async_remote_copy(
                src_ref=w_v.at[pl.ds(32 * d, 32)],
                dst_ref=wr_v.at[1 - d],
                send_sem=w_sem.at[0, d],
                recv_sem=w_sem.at[1, 1 - d],
                device_id=x_dev(x_nb[d]),
                device_id_type=MESH,
            )

        def radiate(t, g, x):
            for p, (re, im) in enumerate(spectrum(x)):
                c = cs_v[0, p : p + 1, :]
                s = cs_v[1, p : p + 1, :]
                both = jnp.concatenate([re * c + im * s, im * c - re * s], axis=0)
                own_v[t, g, 16 * p : 16 * p + 16, :] = both.astype(BF16)
            for d in range(2):
                z_copy(t, g, d).start()

        def partner_sums(t, g):
            for d in range(2):
                z_copy(t, g, d).wait_recv()
            for j in range(4):
                lanes = slice(128 * j, 128 * j + 128)

                def source(row, e):
                    if e < 2:
                        return zr_v[t, g, 0, 16 * (2 * row + e) : 16 * (2 * row + e) + 16, lanes]
                    if e < 4:
                        return own_v[t, g, 16 * (2 * row + e - 2) : 16 * (2 * row + e - 2) + 16, lanes]
                    return zr_v[t, g, 1, 16 * (2 * row + e - 4) : 16 * (2 * row + e - 4) + 16, lanes]

                src = [[source(row, e).astype(F32) for e in range(6)] for row in range(2)]
                for a in range(2):
                    for b in range(2):
                        p = 2 * a + b
                        total = None
                        for row in range(2):
                            for dc in range(5):
                                if row == a and dc == 2:
                                    continue
                                o = (row - a + 1) * 5 + dc
                                w = w_v[16 * p + o : 16 * p + o + 1, :]
                                term = w * src[row][b + dc]
                                total = term if total is None else total + term
                        acc_v[g, 16 * p : 16 * p + 16, lanes] = total
                for d in range(2):
                    row = d
                    for b in range(2):
                        total = None
                        for dc in range(5):
                            o = (10 if d == 0 else 0) + dc
                            w = wr_v[d, 16 * b + o : 16 * b + o + 1, :]
                            term = w * src[row][b + dc]
                            total = term if total is None else total + term
                        push_v[t, g, d, 16 * b : 16 * b + 16, lanes] = total.astype(BF16)
            for d in range(2):
                x_copy(t, g, d).start()

        def receive(t, g):
            for d in range(2):
                x_copy(t, g, d).wait_recv()
            for p in range(4):
                a, b = p // 2, p % 2
                total = acc_v[g, 16 * p : 16 * p + 16, :]
                total = total + pr_v[t, g, a, 16 * b : 16 * b + 16, :].astype(F32)
                re, im = total[0:8], total[8:16]
                c = cs_v[0, p : p + 1, :]
                s = cs_v[1, p : p + 1, :]
                both = jnp.concatenate([re * c - im * s, re * s + im * c], axis=0)
                x_v[16 * p : 16 * p + 16, :] = both.astype(BF16)
            x = x_v[...]
            q0 = jnp.dot(x, radt_v[0], preferred_element_type=F32)
            q1 = jnp.dot(x, radt_v[1], preferred_element_type=F32)
            for p in range(4):
                r, i = 16 * p, 16 * p + 8
                got = jnp.concatenate(
                    [q0[r : r + 8] - q1[i : i + 8], q1[r : r + 8] + q0[i : i + 8]], axis=0
                )
                f = refl_v[p // 2, p % 2 : p % 2 + 1, :]
                new = cinc_v[g, 16 * p : 16 * p + 16, :].astype(F32) + f * got
                curf_v[g, 16 * p : 16 * p + 16, :] = new.astype(BF16)
            return curf_v[g]

        def rs_copy(g, d, peer):
            return pltpu.make_async_remote_copy(
                src_ref=sb_v.at[g, peer],
                dst_ref=rb_v.at[g, d],
                send_sem=rs_sem.at[0, g],
                recv_sem=rs_sem.at[1, g],
                device_id=x_dev(peer),
                device_id_type=MESH,
            )

        def rs_all(g):
            return pltpu.make_async_remote_copy(
                src_ref=sb_v.at[g, pl.ds(0, n_px - 1)],
                dst_ref=rb_v.at[g, pl.ds(1, n_px - 1)],
                send_sem=rs_sem.at[0, g],
                recv_sem=rs_sem.at[1, g],
                device_id=x_dev(x_nb[0]),
                device_id_type=MESH,
            )

        def far_field(g):
            for p, (re, im) in enumerate(spectrum(curf_v[g])):
                both = jnp.concatenate([re, im], axis=0)
                x_v[16 * p : 16 * p + 16, :] = both.astype(BF16)
            x = x_v[...]
            for n in range(4):
                beams = jnp.dot(x, far_v[:, 512 * n : 512 * n + 512], preferred_element_type=F32)
                for m in range(4):
                    u = 4 * n + m
                    at = slice(LN * m, LN * m + LN)
                    far_re = far_im = None
                    for p in range(4):
                        br = beams[16 * p : 16 * p + 8, at]
                        bi = beams[16 * p + 8 : 16 * p + 16, at]
                        c = cv_v[0, p : p + 1, LN * u : LN * u + LN]
                        s = cv_v[1, p : p + 1, LN * u : LN * u + LN]
                        tr = br * c - bi * s
                        ti = br * s + bi * c
                        far_re = tr if far_re is None else far_re + tr
                        far_im = ti if far_im is None else far_im + ti
                    u_v[0, u] = far_re
                    u_v[1, u] = far_im
            spec = fft([(u_v[0, u], u_v[1, u]) for u in range(TW)])
            for t in range(0, TW, 2):
                parts = []
                for tt in (t, t + 1):
                    re, im = spec[tt]
                    if tt:
                        c = tw_v[0, tt : tt + 1, :]
                        s = tw_v[1, tt : tt + 1, :]
                        re, im = re * c + im * s, im * c - re * s
                    parts.append((re, im))
                for part in range(2):
                    y_v[8 * t : 8 * t + 16, LN * part : LN * part + LN] = jnp.concatenate(
                        [parts[0][part], parts[1][part]], axis=0
                    ).astype(BF16)
            bins = lax.dot_general(
                fm_v[...], y_v[...], (((1,), (1,)), ((), ())), preferred_element_type=F32
            )
            sb_v[g] = bins.reshape(n_px, rows_p, LN).astype(BF16)

            def send(d, carry):
                rs_copy(g, d, ring(pi + d, n_px)).start()
                return carry

            lax.fori_loop(1, n_px, send, 0)

        def z_sum_copy(g, owner):
            return pltpu.make_async_remote_copy(
                src_ref=zs_v.at[g],
                dst_ref=zb_v.at[ring(zi - owner, n_z)],
                send_sem=zs_sem.at[0],
                recv_sem=zs_sem.at[1],
                device_id=z_dev(owner),
                device_id_type=MESH,
            )

        def gather_bins(g):
            rs_all(g).wait_recv()
            total = sb_v[g, pi].astype(F32)
            for d in range(1, n_px):
                total = total + rb_v[g, d].astype(F32)
            zs_v[g] = total.astype(BF16)
            for h in range(hz):
                owner = hz * g + h

                @pl.when(zi != owner)
                def _():
                    z_sum_copy(g, owner).start()

        i_part.wait()
        i_cnt.wait()
        i_pw.wait()
        for a in range(2):
            for b in range(2):
                ids = part_v[a, b : b + 1, :]
                row = ids // cols_total
                col = ids - row * cols_total
                dr = row - (2 * pi + a) + 1
                dc = (col - (2 * zi + b) + 2 + cols_total) % cols_total
                slot = lax.broadcasted_iota(jnp.int32, (1, SLOTS), 1)
                live = slot < cnt_v[a : a + 1, b : b + 1]
                w = jnp.where(live, pw_v[a, b : b + 1, :].astype(F32), 0.0)
                kind = dr * 5 + dc
                offsets = lax.broadcasted_iota(jnp.int32, (16, SLOTS), 0)
                table = jnp.where(offsets == kind, jnp.broadcast_to(w, (16, SLOTS)), 0.0)
                column = jnp.sum(table, axis=1, keepdims=True)
                p = 2 * a + b
                w_v[16 * p : 16 * p + 16, :] = jnp.broadcast_to(column, (16, LN))

        pl.semaphore_wait(barrier, 4)
        for d in range(2):
            w_copy(d).start()
        for g in range(G):
            radiate(0, g, cinc_v[g])

        rounds = (
            (zd_sem, z_rounds, z_dev, zi, n_z),
            (xd_sem, x_rounds, x_dev, pi, n_px),
        )

        def tell(n):
            for sem, radii, dev, me, count in rounds:
                if n < len(radii):
                    for side in (-radii[n], radii[n]):
                        pl.semaphore_signal(
                            sem.at[n],
                            inc=1,
                            device_id=dev(ring(me + side, count)),
                            device_id_type=MESH,
                        )

        def hear(n):
            for sem, radii, *_ in rounds:
                if n < len(radii):
                    pl.semaphore_wait(sem.at[n], 2)

        tell(0)

        for part in range(2):
            radt_v[part] = rad_v[part].T
        i_refl.wait()
        i_rd.wait()
        phases(rd_v, cv_v)
        i_tw.wait()
        i_fm.wait()
        i_far.wait()
        for d in range(2):
            w_copy(d).wait_recv()

        partner_sums(0, 0)
        for g in range(G):
            if g + 1 < G:
                partner_sums(0, g + 1)
            radiate(1, g, receive(0, g))
            hear(g)
            tell(g + 1)
        partner_sums(1, 0)
        for g in range(G):
            if g + 1 < G:
                partner_sums(1, g + 1)
            receive(1, g)
            far_field(g)
        for p in range(4):
            for part in range(2):
                whole = jnp.concatenate(
                    [
                        curf_v[g, 16 * p : 16 * p + 16, :].astype(F32)[8 * part : 8 * part + 8]
                        for g in range(G)
                    ],
                    axis=0,
                )
                cur_v[p // 2, p % 2, part] = whole.astype(BF16)
        out = pltpu.make_async_copy(cur_v, cur_h, out_sem)
        out.start()
        for g in range(G):
            gather_bins(g)

        for t in range(2):
            for g in range(G):
                for d in range(2):
                    z_copy(t, g, d).wait_send()
                    x_copy(t, g, d).wait_send()
        for d in range(2):
            w_copy(d).wait_send()
        for g in range(G):
            rs_all(g).wait_send()

        all_z = pltpu.make_async_remote_copy(
            src_ref=zb_v.at[pl.ds(1, n_z - 1)],
            dst_ref=zb_v.at[pl.ds(1, n_z - 1)],
            send_sem=zs_sem.at[0],
            recv_sem=zs_sem.at[1],
            device_id=z_dev(z_nb[0]),
            device_id_type=MESH,
        )
        all_z.wait_recv()
        total = zs_v[zi // hz].astype(F32)
        for d in range(1, n_z):
            total = total + zb_v[d].astype(F32)
        power = total * total
        power = (power[0:qp] + power[qp : 2 * qp]) * scale
        if qp < 8:
            power = jnp.concatenate([power, jnp.zeros((8 - qp, LN), F32)], axis=0)
        width = TW * qp
        lane = lax.broadcasted_iota(jnp.int32, (LN, width), 0)
        bin_id = lax.broadcasted_iota(jnp.int32, (LN, width), 1)
        row_id = lax.broadcasted_iota(jnp.int32, (max(qp, 8), width), 0)
        bin_row = lax.broadcasted_iota(jnp.int32, (max(qp, 8), width), 1) // TW
        first = lax.rem(zi, hz) * kz
        for b in range(kz):
            pick = jnp.where(lane == (bin_id % TW) * KC + first + b, 1.0, 0.0)
            rows = jnp.dot(power, pick, precision=lax.Precision.HIGHEST, preferred_element_type=F32)
            img_o[b : b + 1, :] = jnp.sum(
                jnp.where(row_id == bin_row, rows, 0.0), axis=0, keepdims=True
            )
        all_z.wait_send()
        out.wait()

    return kernel


def tables(n_px):
    qp = LN // n_px
    row = np.arange(2 * LN)
    part_out = (row // qp) % 2
    q = (row // (2 * qp)) * qp + row % qp
    col = np.arange(2 * LN)
    part_in, v = col // LN, col % LN
    turn = (q[:, None] * v[None, :] + (LN // 4) * (part_out[:, None] - part_in[None, :])) % LN
    second = np.cos(2 * math.pi * turn / LN).astype(np.float32)
    angle = 2 * math.pi * np.arange(TW)[:, None] * np.arange(LN)[None, :] / (TW * LN)
    twiddle = np.stack([np.cos(angle), np.sin(angle)]).astype(np.float32)
    return second, twiddle


def solution(mesh):
    n_px, n_z = mesh.shape["px"], mesh.shape["py"]

    def local(cin, rad, far, refl, cen, sd, rd, part, cnt, pw):
        illum, units = cin.shape[3], cin.shape[4]
        rcv = rd.shape[1]
        dirs = sd.shape[1]
        second, twiddle = tables(n_px)
        qp = LN // n_px
        kz = illum // n_z
        kernel = make_kernel(n_px, n_z, illum, rcv)
        V = pltpu.VMEM
        dma = pltpu.SemaphoreType.DMA
        regular = pltpu.SemaphoreType.REGULAR
        scratch = [
            V(cin.shape, BF16),
            V(rad.shape, BF16),
            V((2, dirs, units), BF16),
            V(far.shape, BF16),
            V(refl.shape, F32),
            V(cen.shape, F32),
            V(sd.shape, F32),
            V(rd.shape, F32),
            V(part.shape, jnp.int32),
            V(cnt.shape, jnp.int32),
            V(pw.shape, BF16),
            V((2 * LN, 2 * LN), BF16),
            V((2, TW, LN), F32),
            V((64, LN), F32),
            V((2, 32, LN), F32),
            V((2, 8, dirs), F32),
            V((2, 8, rcv), F32),
            V((G, 64, units), BF16),
            V((64, units), BF16),
            V((2, G, 64, dirs), BF16),
            V((2, G, 2, 64, dirs), BF16),
            V((G, 64, dirs), F32),
            V((2, G, 2, 32, dirs), BF16),
            V((2, G, 2, 32, dirs), BF16),
            V((G, 64, units), BF16),
            V((2, TW, KC, LN), F32),
            V((LN, 2 * LN), BF16),
            V((G, n_px, 2 * qp, LN), BF16),
            V((G, n_px, 2 * qp, LN), BF16),
            V((G, 2 * qp, LN), BF16),
            V((n_z, 2 * qp, LN), BF16),
            V(cin.shape, BF16),
            dma((12,)),
            dma((2, 2)),
            dma((2, 2, G, 2)),
            dma((2, 2, G, 2)),
            dma((2, G)),
            dma((2,)),
            dma,
            regular((max(1, len(doubling(n_z))),)),
            regular((max(1, len(doubling(n_px))),)),
        ]
        return pl.pallas_call(
            kernel,
            out_shape=(
                jax.ShapeDtypeStruct(cin.shape, BF16),
                jax.ShapeDtypeStruct((kz, TW * qp), F32),
            ),
            in_specs=[pl.BlockSpec(memory_space=pl.ANY)] * 12,
            out_specs=(
                pl.BlockSpec(memory_space=pl.ANY),
                pl.BlockSpec(memory_space=pltpu.VMEM),
            ),
            scratch_shapes=scratch,
            compiler_params=pltpu.CompilerParams(
                collective_id=0, has_side_effects=True, vmem_limit_bytes=48 << 20
            ),
        )(
            cin, rad, far, refl, cen, sd, rd, part, cnt, pw,
            jnp.asarray(second, BF16), jnp.asarray(twiddle),
        )

    in_specs = (
        P("px", "py", None, None, None),
        P(),
        P(),
        P("px", "py", None),
        P(None, "px", "py"),
        P(),
        P(),
        P("px", "py", None),
        P("px", "py"),
        P("px", "py", None),
    )
    out_specs = (P("px", "py", None, None, None), P("py", "px"))
    return jax.shard_map(local, mesh=mesh, in_specs=in_specs, out_specs=out_specs, check_vma=False)
```

```python
import math

import numpy as np

import jax
import jax.numpy as jnp
from jax import lax
from jax.experimental import pallas as pl
from jax.experimental.pallas import tpu as pltpu
from jax.sharding import PartitionSpec as P

MESH = pl.DeviceIdType.MESH
F32 = jnp.float32
BF16 = jnp.bfloat16
SLOTS = 12
G = 4
KC = 8
TW = 16
LN = 128


def fft(values):
    size = len(values)
    if size == 1:
        return values
    even = fft(values[0::2])
    odd = fft(values[1::2])
    low, high = [], []
    for t in range(size // 2):
        re, im = odd[t]
        if t == 0:
            pass
        elif 4 * t == size:
            re, im = im, -re
        else:
            c = math.cos(2 * math.pi * t / size)
            s = math.sin(2 * math.pi * t / size)
            if 8 * t == size:
                re, im = (re + im) * c, (im - re) * c
            elif 8 * t == 3 * size:
                re, im = (im - re) * s, (re + im) * (-s)
            else:
                re, im = re * c + im * s, im * c - re * s
        er, ei = even[t]
        low.append((er + re, ei + im))
        high.append((er - re, ei - im))
    return low + high


def doubling(reach):
    radii, radius = [], 1
    while radius < reach:
        radii.append(radius)
        radius *= 2
    return radii


def make_kernel(n_px, n_z, illum, rcv):
    cols_total = 2 * n_z
    patches = 4 * n_px * n_z
    qp = LN // n_px
    rows_p = 2 * qp
    kz = illum // n_z
    hz = KC // kz
    z_rounds = doubling(n_z // 2)
    x_rounds = doubling(n_px - 1)
    scale = 0.125 / (patches * rcv)

    def kernel(
        cin_h, rad_h, far_h, refl_h, cen_h, sd_h, rd_h, part_h, cnt_h, pw_h, fm_h, tw_h,
        cur_o, img_o,
        cin_v, rad_v, radt_v, far_v, refl_v, cen_v, sd_v, rd_v, part_v, cnt_v, pw_v, fm_v, tw_v,
        w_v, wr_v, cs_v, cv_v, cinc_v, x_v, own_v, zr_v, acc_v, push_v, pr_v, curf_v,
        u_v, y_v, sb_v, rb_v, zs_v, zb_v,
        in_sem, w_sem, zx_sem, px_sem, rs_sem, zs_sem, zd_sem, xd_sem,
    ):
        pi = lax.axis_index("px")
        zi = lax.axis_index("py")

        def ring(value, count):
            return lax.rem(value + count, count)

        z_nb = (ring(zi - 1, n_z), ring(zi + 1, n_z))
        x_nb = (ring(pi - 1, n_px), ring(pi + 1, n_px))
        has_x = (pi > 0, pi < n_px - 1)

        def z_dev(z):
            return (pi, z)

        def x_dev(x):
            return (x, zi)

        barrier = pltpu.get_barrier_semaphore()
        for z in z_nb:
            pl.semaphore_signal(barrier, inc=1, device_id=z_dev(z), device_id_type=MESH)
        for d in range(2):

            @pl.when(has_x[d])
            def _():
                pl.semaphore_signal(barrier, inc=1, device_id=x_dev(x_nb[d]), device_id_type=MESH)


        ins = []
        for n, (src, dst) in enumerate(
            (
                (sd_h, sd_v), (cen_h, cen_v), (part_h, part_v), (cnt_h, cnt_v),
                (pw_h, pw_v), (cin_h, cin_v), (rad_h, rad_v), (refl_h, refl_v),
                (rd_h, rd_v), (tw_h, tw_v), (fm_h, fm_v), (far_h, far_v),
            )
        ):
            copy = pltpu.make_async_copy(src, dst, in_sem.at[n])
            copy.start()
            ins.append(copy)
        (i_sd, i_cen, i_part, i_cnt, i_pw, i_cin, i_rad, i_refl, i_rd, i_tw, i_fm, i_far) = ins

        def phases(dirs, out):
            for a in range(2):
                for b in range(2):
                    total = None
                    for d in range(3):
                        term = dirs[d : d + 1, :] * cen_v[a, b : b + 1, d : d + 1]
                        total = term if total is None else total + term
                    out[0, 2 * a + b : 2 * a + b + 1, :] = total
            phi = out[0, 0:4, :]
            out[0, 0:4, :] = jnp.cos(phi)
            out[1, 0:4, :] = jnp.sin(phi)

        for d in range(2):

            @pl.when(jnp.logical_not(has_x[d]))
            def _():
                wr_v[d] = jnp.zeros(wr_v.shape[1:], F32)
                for t in range(2):
                    for g in range(G):
                        pr_v[t, g, d] = jnp.zeros(pr_v.shape[3:], BF16)

        i_sd.wait()
        i_cen.wait()
        phases(sd_v, cs_v)

        i_cin.wait()
        for p in range(4):
            x0 = cin_v[p // 2, p % 2, 0].astype(F32)
            x1 = cin_v[p // 2, p % 2, 1].astype(F32)
            for g in range(G):
                both = jnp.concatenate([x0[KC * g : KC * g + KC], x1[KC * g : KC * g + KC]], axis=0)
                cinc_v[g, 16 * p : 16 * p + 16, :] = both.astype(BF16)
        i_rad.wait()

        def spectrum(x):
            x0 = jnp.dot(x, rad_v[0], preferred_element_type=F32)
            x1 = jnp.dot(x, rad_v[1], preferred_element_type=F32)
            out = []
            for p in range(4):
                r, i = 16 * p, 16 * p + 8
                out.append((x0[r : r + 8] - x1[i : i + 8], x1[r : r + 8] + x0[i : i + 8]))
            return out

        def z_copy(t, g, d):
            return pltpu.make_async_remote_copy(
                src_ref=own_v.at[t, g],
                dst_ref=zr_v.at[t, g, 1 - d],
                send_sem=zx_sem.at[0, t, g, d],
                recv_sem=zx_sem.at[1, t, g, 1 - d],
                device_id=z_dev(z_nb[d]),
                device_id_type=MESH,
            )

        def x_copy(t, g, d):
            return pltpu.make_async_remote_copy(
                src_ref=push_v.at[t, g, d],
                dst_ref=pr_v.at[t, g, 1 - d],
                send_sem=px_sem.at[0, t, g, d],
                recv_sem=px_sem.at[1, t, g, 1 - d],
                device_id=x_dev(x_nb[d]),
                device_id_type=MESH,
            )

        def w_copy(d):
            return pltpu.make_async_remote_copy(
                src_ref=w_v.at[pl.ds(32 * d, 32)],
                dst_ref=wr_v.at[1 - d],
                send_sem=w_sem.at[0, d],
                recv_sem=w_sem.at[1, 1 - d],
                device_id=x_dev(x_nb[d]),
                device_id_type=MESH,
            )

        def radiate(t, g, x):
            for p, (re, im) in enumerate(spectrum(x)):
                c = cs_v[0, p : p + 1, :]
                s = cs_v[1, p : p + 1, :]
                both = jnp.concatenate([re * c + im * s, im * c - re * s], axis=0)
                own_v[t, g, 16 * p : 16 * p + 16, :] = both.astype(BF16)
            for d in range(2):
                z_copy(t, g, d).start()

        def partner_sums(t, g):
            for d in range(2):
                z_copy(t, g, d).wait_recv()
            for j in range(4):
                lanes = slice(128 * j, 128 * j + 128)

                def source(row, e):
                    if e < 2:
                        return zr_v[t, g, 0, 16 * (2 * row + e) : 16 * (2 * row + e) + 16, lanes]
                    if e < 4:
                        return own_v[t, g, 16 * (2 * row + e - 2) : 16 * (2 * row + e - 2) + 16, lanes]
                    return zr_v[t, g, 1, 16 * (2 * row + e - 4) : 16 * (2 * row + e - 4) + 16, lanes]

                src = [[source(row, e).astype(F32) for e in range(6)] for row in range(2)]
                for a in range(2):
                    for b in range(2):
                        p = 2 * a + b
                        total = None
                        for row in range(2):
                            for dc in range(5):
                                if row == a and dc == 2:
                                    continue
                                o = (row - a + 1) * 5 + dc
                                w = w_v[16 * p + o : 16 * p + o + 1, :]
                                term = w * src[row][b + dc]
                                total = term if total is None else total + term
                        acc_v[g, 16 * p : 16 * p + 16, lanes] = total
                for d in range(2):
                    row = d
                    for b in range(2):
                        total = None
                        for dc in range(5):
                            o = (10 if d == 0 else 0) + dc
                            w = wr_v[d, 16 * b + o : 16 * b + o + 1, :]
                            term = w * src[row][b + dc]
                            total = term if total is None else total + term
                        push_v[t, g, d, 16 * b : 16 * b + 16, lanes] = total.astype(BF16)
            for d in range(2):

                @pl.when(has_x[d])
                def _():
                    x_copy(t, g, d).start()


        def receive(t, g):
            for d in range(2):

                @pl.when(has_x[d])
                def _():
                    x_copy(t, g, 1 - d).wait_recv()

            for p in range(4):
                a, b = p // 2, p % 2
                total = acc_v[g, 16 * p : 16 * p + 16, :]
                total = total + pr_v[t, g, a, 16 * b : 16 * b + 16, :].astype(F32)
                re, im = total[0:8], total[8:16]
                c = cs_v[0, p : p + 1, :]
                s = cs_v[1, p : p + 1, :]
                both = jnp.concatenate([re * c - im * s, re * s + im * c], axis=0)
                x_v[16 * p : 16 * p + 16, :] = both.astype(BF16)
            x = x_v[...]
            q0 = jnp.dot(x, radt_v[0], preferred_element_type=F32)
            q1 = jnp.dot(x, radt_v[1], preferred_element_type=F32)
            for p in range(4):
                r, i = 16 * p, 16 * p + 8
                got = jnp.concatenate(
                    [q0[r : r + 8] - q1[i : i + 8], q1[r : r + 8] + q0[i : i + 8]], axis=0
                )
                f = refl_v[p // 2, p % 2 : p % 2 + 1, :]
                new = cinc_v[g, 16 * p : 16 * p + 16, :].astype(F32) + f * got
                curf_v[g, 16 * p : 16 * p + 16, :] = new.astype(BF16)
            return curf_v[g]

        def rs_copy(g, d, peer):
            return pltpu.make_async_remote_copy(
                src_ref=sb_v.at[g, peer],
                dst_ref=rb_v.at[g, d],
                send_sem=rs_sem.at[0, g],
                recv_sem=rs_sem.at[1, g],
                device_id=x_dev(peer),
                device_id_type=MESH,
            )

        def rs_all(g):
            return pltpu.make_async_remote_copy(
                src_ref=sb_v.at[g, pl.ds(0, n_px - 1)],
                dst_ref=rb_v.at[g, pl.ds(1, n_px - 1)],
                send_sem=rs_sem.at[0, g],
                recv_sem=rs_sem.at[1, g],
                device_id=x_dev(ring(pi + 1, n_px)),
                device_id_type=MESH,
            )

        def far_field(g):
            for p, (re, im) in enumerate(spectrum(curf_v[g])):
                both = jnp.concatenate([re, im], axis=0)
                x_v[16 * p : 16 * p + 16, :] = both.astype(BF16)
            x = x_v[...]
            for n in range(4):
                beams = jnp.dot(x, far_v[:, 512 * n : 512 * n + 512], preferred_element_type=F32)
                for m in range(4):
                    u = 4 * n + m
                    at = slice(LN * m, LN * m + LN)
                    far_re = far_im = None
                    for p in range(4):
                        br = beams[16 * p : 16 * p + 8, at]
                        bi = beams[16 * p + 8 : 16 * p + 16, at]
                        c = cv_v[0, p : p + 1, LN * u : LN * u + LN]
                        s = cv_v[1, p : p + 1, LN * u : LN * u + LN]
                        tr = br * c - bi * s
                        ti = br * s + bi * c
                        far_re = tr if far_re is None else far_re + tr
                        far_im = ti if far_im is None else far_im + ti
                    u_v[0, u] = far_re
                    u_v[1, u] = far_im
            spec = fft([(u_v[0, u], u_v[1, u]) for u in range(TW)])
            for t in range(0, TW, 2):
                parts = []
                for tt in (t, t + 1):
                    re, im = spec[tt]
                    if tt:
                        c = tw_v[0, tt : tt + 1, :]
                        s = tw_v[1, tt : tt + 1, :]
                        re, im = re * c + im * s, im * c - re * s
                    parts.append((re, im))
                for part in range(2):
                    y_v[8 * t : 8 * t + 16, LN * part : LN * part + LN] = jnp.concatenate(
                        [parts[0][part], parts[1][part]], axis=0
                    ).astype(BF16)
            bins = lax.dot_general(
                fm_v[...], y_v[...], (((1,), (1,)), ((), ())), preferred_element_type=F32
            )
            sb_v[g] = bins.reshape(n_px, rows_p, LN).astype(BF16)

            def send(d, carry):
                rs_copy(g, d, ring(pi + d, n_px)).start()
                return carry

            lax.fori_loop(1, n_px, send, 0)

        def z_sum_copy(g, owner):
            return pltpu.make_async_remote_copy(
                src_ref=zs_v.at[g],
                dst_ref=zb_v.at[ring(zi - owner, n_z)],
                send_sem=zs_sem.at[0],
                recv_sem=zs_sem.at[1],
                device_id=z_dev(owner),
                device_id_type=MESH,
            )

        def gather_bins(g):
            rs_all(g).wait_recv()
            total = sb_v[g, pi].astype(F32)
            for d in range(1, n_px):
                total = total + rb_v[g, d].astype(F32)
            zs_v[g] = total.astype(BF16)
            for h in range(hz):
                owner = hz * g + h

                @pl.when(zi != owner)
                def _():
                    z_sum_copy(g, owner).start()

        i_part.wait()
        i_cnt.wait()
        i_pw.wait()
        for a in range(2):
            for b in range(2):
                ids = part_v[a, b : b + 1, :]
                row = ids // cols_total
                col = ids - row * cols_total
                dr = row - (2 * pi + a) + 1
                dc = (col - (2 * zi + b) + 2 + cols_total) % cols_total
                slot = lax.broadcasted_iota(jnp.int32, (1, SLOTS), 1)
                live = slot < cnt_v[a : a + 1, b : b + 1]
                w = jnp.where(live, pw_v[a, b : b + 1, :].astype(F32), 0.0)
                kind = dr * 5 + dc
                offsets = lax.broadcasted_iota(jnp.int32, (16, SLOTS), 0)
                table = jnp.where(offsets == kind, jnp.broadcast_to(w, (16, SLOTS)), 0.0)
                column = jnp.sum(table, axis=1, keepdims=True)
                p = 2 * a + b
                w_v[16 * p : 16 * p + 16, :] = jnp.broadcast_to(column, (16, LN))

        pl.semaphore_wait(barrier, 2 + (pi > 0).astype(jnp.int32) + (pi < n_px - 1).astype(jnp.int32))
        for d in range(2):

            @pl.when(has_x[d])
            def _():
                w_copy(d).start()

        for g in range(G):
            radiate(0, g, cinc_v[g])

        def z_tell(n):
            if n < len(z_rounds):
                for side in (-z_rounds[n], z_rounds[n]):
                    pl.semaphore_signal(
                        zd_sem.at[n], inc=1, device_id=z_dev(ring(zi + side, n_z)), device_id_type=MESH
                    )

        def z_hear(n):
            if n < len(z_rounds):
                pl.semaphore_wait(zd_sem.at[n], 2)

        def x_tell(n):
            if n < len(x_rounds):
                for side in (-x_rounds[n], x_rounds[n]):
                    other = pi + side

                    @pl.when((other >= 0) & (other < n_px))
                    def _():
                        pl.semaphore_signal(
                            xd_sem.at[n], inc=1, device_id=x_dev(other), device_id_type=MESH
                        )

        def x_hear(n):
            if n < len(x_rounds):
                low = (pi - x_rounds[n] >= 0).astype(jnp.int32)
                high = (pi + x_rounds[n] < n_px).astype(jnp.int32)
                pl.semaphore_wait(xd_sem.at[n], low + high)

        z_tell(0)
        x_tell(0)

        for part in range(2):
            radt_v[part] = rad_v[part].T
        i_refl.wait()
        i_rd.wait()
        phases(rd_v, cv_v)
        i_tw.wait()
        i_fm.wait()
        i_far.wait()
        for d in range(2):

            @pl.when(has_x[d])
            def _():
                w_copy(1 - d).wait_recv()

        x_hear(0)
        x_tell(1)
        for g in range(G):
            partner_sums(0, g)
        x_hear(1)
        x_tell(2)
        z_hear(0)
        z_tell(1)
        for g in range(G):
            radiate(1, g, receive(0, g))
        x_hear(2)
        x_tell(3)
        z_hear(1)
        z_tell(2)
        for g in range(G):
            partner_sums(1, g)
            if g == 0:
                x_hear(3)
                x_tell(4)
        for g in range(G):
            receive(1, g)
            if g == 0:
                x_hear(4)
            far_field(g)
        z_hear(2)
        for p in range(4):
            for part in range(2):
                whole = jnp.concatenate(
                    [
                        curf_v[g, 16 * p : 16 * p + 16, :].astype(F32)[8 * part : 8 * part + 8]
                        for g in range(G)
                    ],
                    axis=0,
                )
                cur_o[p // 2, p % 2, part] = whole.astype(BF16)
        for g in range(G):
            gather_bins(g)

        for t in range(2):
            for g in range(G):
                for d in range(2):
                    z_copy(t, g, d).wait_send()
        for d in range(2):

            @pl.when(has_x[d])
            def _():
                w_copy(d).wait_send()
                for t in range(2):
                    for g in range(G):
                        x_copy(t, g, d).wait_send()

        for g in range(G):
            rs_all(g).wait_send()

        all_z = pltpu.make_async_remote_copy(
            src_ref=zb_v.at[pl.ds(1, n_z - 1)],
            dst_ref=zb_v.at[pl.ds(1, n_z - 1)],
            send_sem=zs_sem.at[0],
            recv_sem=zs_sem.at[1],
            device_id=z_dev(z_nb[0]),
            device_id_type=MESH,
        )
        all_z.wait_recv()
        total = zs_v[zi // hz].astype(F32)
        for d in range(1, n_z):
            total = total + zb_v[d].astype(F32)
        power = total * total
        power = (power[0:qp] + power[qp : 2 * qp]) * scale
        if qp < 8:
            power = jnp.concatenate([power, jnp.zeros((8 - qp, LN), F32)], axis=0)
        width = TW * qp
        lane = lax.broadcasted_iota(jnp.int32, (LN, width), 0)
        bin_id = lax.broadcasted_iota(jnp.int32, (LN, width), 1)
        row_id = lax.broadcasted_iota(jnp.int32, (max(qp, 8), width), 0)
        bin_row = lax.broadcasted_iota(jnp.int32, (max(qp, 8), width), 1) // TW
        first = lax.rem(zi, hz) * kz
        for b in range(kz):
            pick = jnp.where(lane == (bin_id % TW) * KC + first + b, 1.0, 0.0)
            rows = jnp.dot(power, pick, precision=lax.Precision.HIGHEST, preferred_element_type=F32)
            img_o[b : b + 1, :] = jnp.sum(
                jnp.where(row_id == bin_row, rows, 0.0), axis=0, keepdims=True
            )
        all_z.wait_send()

    return kernel


def tables(n_px):
    qp = LN // n_px
    row = np.arange(2 * LN)
    part_out = (row // qp) % 2
    q = (row // (2 * qp)) * qp + row % qp
    col = np.arange(2 * LN)
    part_in, v = col // LN, col % LN
    turn = (q[:, None] * v[None, :] + (LN // 4) * (part_out[:, None] - part_in[None, :])) % LN
    second = np.cos(2 * math.pi * turn / LN).astype(np.float32)
    angle = 2 * math.pi * np.arange(TW)[:, None] * np.arange(LN)[None, :] / (TW * LN)
    twiddle = np.stack([np.cos(angle), np.sin(angle)]).astype(np.float32)
    return second, twiddle


def solution(mesh):
    n_px, n_z = mesh.shape["px"], mesh.shape["py"]

    def local(cin, rad, far, refl, cen, sd, rd, part, cnt, pw):
        illum, units = cin.shape[3], cin.shape[4]
        rcv = rd.shape[1]
        dirs = sd.shape[1]
        second, twiddle = tables(n_px)
        qp = LN // n_px
        kz = illum // n_z
        kernel = make_kernel(n_px, n_z, illum, rcv)
        V = pltpu.VMEM
        dma = pltpu.SemaphoreType.DMA
        regular = pltpu.SemaphoreType.REGULAR
        scratch = [
            V(cin.shape, BF16),
            V(rad.shape, BF16),
            V((2, dirs, units), BF16),
            V(far.shape, BF16),
            V(refl.shape, F32),
            V((2, 2, 3), F32),
            V(sd.shape, F32),
            V(rd.shape, F32),
            V(part.shape, jnp.int32),
            V(cnt.shape, jnp.int32),
            V(pw.shape, BF16),
            V((2 * LN, 2 * LN), BF16),
            V((2, TW, LN), F32),
            V((64, LN), F32),
            V((2, 32, LN), F32),
            V((2, 8, dirs), F32),
            V((2, 8, rcv), F32),
            V((G, 64, units), BF16),
            V((64, units), BF16),
            V((2, G, 64, dirs), BF16),
            V((2, G, 2, 64, dirs), BF16),
            V((G, 64, dirs), F32),
            V((2, G, 2, 32, dirs), BF16),
            V((2, G, 2, 32, dirs), BF16),
            V((G, 64, units), BF16),
            V((2, TW, KC, LN), F32),
            V((LN, 2 * LN), BF16),
            V((G, n_px, 2 * qp, LN), BF16),
            V((G, n_px, 2 * qp, LN), BF16),
            V((G, 2 * qp, LN), BF16),
            V((n_z, 2 * qp, LN), BF16),
            dma((12,)),
            dma((2, 2)),
            dma((2, 2, G, 2)),
            dma((2, 2, G, 2)),
            dma((2, G)),
            dma((2,)),
            regular((max(1, len(doubling(n_z // 2))),)),
            regular((max(1, len(doubling(n_px - 1))),)),
        ]
        return pl.pallas_call(
            kernel,
            out_shape=(
                pltpu.VMEM(cin.shape, BF16),
                pltpu.VMEM((kz, TW * qp), F32),
            ),
            in_specs=[pl.BlockSpec(memory_space=pltpu.HBM)] * 12,
            out_specs=(
                pl.BlockSpec(memory_space=pltpu.VMEM),
                pl.BlockSpec(memory_space=pltpu.VMEM),
            ),
            scratch_shapes=scratch,
            compiler_params=pltpu.CompilerParams(
                collective_id=0, has_side_effects=True, vmem_limit_bytes=60 << 20
            ),
        )(
            cin, rad, far, refl, jnp.transpose(cen, (1, 2, 0)), sd, rd, part, cnt, pw,
            jnp.asarray(second, BF16), jnp.asarray(twiddle),
        )

    in_specs = (
        P("px", "py", None, None, None),
        P(),
        P(),
        P("px", "py", None),
        P(None, "px", "py"),
        P(),
        P(),
        P("px", "py", None),
        P("px", "py"),
        P("px", "py", None),
    )
    out_specs = (P("px", "py", None, None, None), P("py", "px"))
    return jax.shard_map(local, mesh=mesh, in_specs=in_specs, out_specs=out_specs, check_vma=False)
```

```python
import math

import numpy as np

import jax
import jax.numpy as jnp
from jax import lax
from jax.experimental import pallas as pl
from jax.experimental.pallas import tpu as pltpu
from jax.sharding import PartitionSpec as P

MESH = pl.DeviceIdType.MESH
F32 = jnp.float32
BF16 = jnp.bfloat16
SLOTS = 12
G = 4
KC = 8
TW = 16
LN = 128


def fft(values):
    size = len(values)
    if size == 1:
        return values
    even = fft(values[0::2])
    odd = fft(values[1::2])
    low, high = [], []
    for t in range(size // 2):
        re, im = odd[t]
        if t == 0:
            pass
        elif 4 * t == size:
            re, im = im, -re
        else:
            c = math.cos(2 * math.pi * t / size)
            s = math.sin(2 * math.pi * t / size)
            if 8 * t == size:
                re, im = (re + im) * c, (im - re) * c
            elif 8 * t == 3 * size:
                re, im = (im - re) * s, (re + im) * (-s)
            else:
                re, im = re * c + im * s, im * c - re * s
        er, ei = even[t]
        low.append((er + re, ei + im))
        high.append((er - re, ei - im))
    return low + high


def doubling(reach):
    radii, radius = [], 1
    while radius < reach:
        radii.append(radius)
        radius *= 2
    return radii


def make_kernel(n_px, n_z, illum, rcv):
    cols_total = 2 * n_z
    patches = 4 * n_px * n_z
    qp = LN // n_px
    rows_p = 2 * qp
    kz = illum // n_z
    hz = KC // kz
    z_rounds = doubling(n_z // 2)
    x_rounds = doubling(n_px - 1)
    scale = 0.125 / (patches * rcv)

    def kernel(
        cin_h, rad_h, far_h, refl_h, cen_h, sd_h, rd_h, part_h, cnt_h, pw_h, fm_h, tw_h,
        cur_o, img_o,
        cin_v, rad_v, radt_v, far_v, refl_v, cen_v, sd_v, rd_v, part_v, cnt_v, pw_v, fm_v, tw_v,
        w_v, wr_v, nrefl_v, ncen_v, cs_v, cv_v, cinc_v, x_v, own_v, zr_v, acc_v, push_v, pr_v, curf_v,
        u_v, xf_v, y_v, sb_v, rb_v, zs_v, zb_v,
        in_sem, w_sem, n_sem, zx_sem, px_sem, rs_sem, zs_sem, zd_sem, xd_sem,
    ):
        pi = lax.axis_index("px")
        zi = lax.axis_index("py")

        def ring(value, count):
            return lax.rem(value + count, count)

        z_nb = (ring(zi - 1, n_z), ring(zi + 1, n_z))
        x_nb = (ring(pi - 1, n_px), ring(pi + 1, n_px))
        has_x = (pi > 0, pi < n_px - 1)

        def z_dev(z):
            return (pi, z)

        def x_dev(x):
            return (x, zi)

        barrier = pltpu.get_barrier_semaphore()
        for z in z_nb:
            pl.semaphore_signal(barrier, inc=1, device_id=z_dev(z), device_id_type=MESH)
        for d in range(2):

            @pl.when(has_x[d])
            def _():
                pl.semaphore_signal(barrier, inc=1, device_id=x_dev(x_nb[d]), device_id_type=MESH)


        ins = []
        for n, (src, dst) in enumerate(
            (
                (sd_h, sd_v), (cen_h, cen_v), (part_h, part_v), (cnt_h, cnt_v),
                (pw_h, pw_v), (cin_h, cin_v), (rad_h, rad_v), (refl_h, refl_v),
                (rd_h, rd_v), (tw_h, tw_v), (fm_h, fm_v), (far_h, far_v),
            )
        ):
            copy = pltpu.make_async_copy(src, dst, in_sem.at[n])
            if n < 7:
                copy.start()
            ins.append(copy)
        (i_sd, i_cen, i_part, i_cnt, i_pw, i_cin, i_rad, i_refl, i_rd, i_tw, i_fm, i_far) = ins

        def phases(dirs, out, cen, first):
            for n in range(4):
                total = None
                for d in range(3):
                    term = dirs[d : d + 1, :] * cen[n // 2, n % 2 : n % 2 + 1, d : d + 1]
                    total = term if total is None else total + term
                out[0, first + n : first + n + 1, :] = total
            phi = out[0, first : first + 4, :]
            out[0, first : first + 4, :] = jnp.cos(phi)
            out[1, first : first + 4, :] = jnp.sin(phi)

        for d in range(2):

            @pl.when(jnp.logical_not(has_x[d]))
            def _():
                wr_v[d] = jnp.zeros(wr_v.shape[1:], F32)
                nrefl_v[d] = jnp.zeros(nrefl_v.shape[1:], F32)
                ncen_v[d] = jnp.zeros(ncen_v.shape[1:], F32)
                for t in range(2):
                    for g in range(G):
                        pr_v[t, g, d] = jnp.zeros(pr_v.shape[3:], BF16)

        i_sd.wait()
        i_cen.wait()
        phases(sd_v, cs_v, cen_v, 0)

        i_cin.wait()
        for p in range(4):
            x0 = cin_v[p // 2, p % 2, 0].astype(F32)
            x1 = cin_v[p // 2, p % 2, 1].astype(F32)
            for g in range(G):
                both = jnp.concatenate([x0[KC * g : KC * g + KC], x1[KC * g : KC * g + KC]], axis=0)
                cinc_v[g, 16 * p : 16 * p + 16, :] = both.astype(BF16)
        i_rad.wait()

        def spectrum(x):
            x0 = jnp.dot(x, rad_v[0], preferred_element_type=F32)
            x1 = jnp.dot(x, rad_v[1], preferred_element_type=F32)
            out = []
            for p in range(x.shape[0] // 16):
                r, i = 16 * p, 16 * p + 8
                out.append((x0[r : r + 8] - x1[i : i + 8], x1[r : r + 8] + x0[i : i + 8]))
            return out

        def z_copy(t, g, d):
            return pltpu.make_async_remote_copy(
                src_ref=own_v.at[t, g],
                dst_ref=zr_v.at[t, g, 1 - d],
                send_sem=zx_sem.at[0, t, g, d],
                recv_sem=zx_sem.at[1, t, g, 1 - d],
                device_id=z_dev(z_nb[d]),
                device_id_type=MESH,
            )

        def x_copy(t, g, d):
            return pltpu.make_async_remote_copy(
                src_ref=push_v.at[t, g, d],
                dst_ref=pr_v.at[t, g, 1 - d],
                send_sem=px_sem.at[0, t, g, d],
                recv_sem=px_sem.at[1, t, g, 1 - d],
                device_id=x_dev(x_nb[d]),
                device_id_type=MESH,
            )

        def w_copy(d):
            return pltpu.make_async_remote_copy(
                src_ref=w_v.at[pl.ds(32 * d, 32)],
                dst_ref=wr_v.at[1 - d],
                send_sem=w_sem.at[0, d],
                recv_sem=w_sem.at[1, 1 - d],
                device_id=x_dev(x_nb[d]),
                device_id_type=MESH,
            )

        def n_copies(d):
            return [
                pltpu.make_async_remote_copy(
                    src_ref=src.at[d],
                    dst_ref=dst.at[1 - d],
                    send_sem=n_sem.at[0, n, d],
                    recv_sem=n_sem.at[1, n, 1 - d],
                    device_id=x_dev(x_nb[d]),
                    device_id_type=MESH,
                )
                for n, (src, dst) in enumerate(((refl_v, nrefl_v), (cen_v, ncen_v)))
            ]

        def radiate(t, g, x):
            for p, (re, im) in enumerate(spectrum(x)):
                c = cs_v[0, p : p + 1, :]
                s = cs_v[1, p : p + 1, :]
                both = jnp.concatenate([re * c + im * s, im * c - re * s], axis=0)
                own_v[t, g, 16 * p : 16 * p + 16, :] = both.astype(BF16)
            for d in range(2):
                z_copy(t, g, d).start()

        def partner_sums(t, g):
            for d in range(2):
                z_copy(t, g, d).wait_recv()
            for j in range(4):
                lanes = slice(128 * j, 128 * j + 128)

                def source(row, e):
                    if e < 2:
                        return zr_v[t, g, 0, 16 * (2 * row + e) : 16 * (2 * row + e) + 16, lanes]
                    if e < 4:
                        return own_v[t, g, 16 * (2 * row + e - 2) : 16 * (2 * row + e - 2) + 16, lanes]
                    return zr_v[t, g, 1, 16 * (2 * row + e - 4) : 16 * (2 * row + e - 4) + 16, lanes]

                src = [[source(row, e).astype(F32) for e in range(6)] for row in range(2)]
                for a in range(2):
                    for b in range(2):
                        p = 2 * a + b
                        total = None
                        for row in range(2):
                            for dc in range(5):
                                if row == a and dc == 2:
                                    continue
                                o = (row - a + 1) * 5 + dc
                                w = w_v[16 * p + o : 16 * p + o + 1, :]
                                term = w * src[row][b + dc]
                                total = term if total is None else total + term
                        acc_v[g, 16 * p : 16 * p + 16, lanes] = total
                for d in range(2):
                    row = d
                    for b in range(2):
                        total = None
                        for dc in range(5):
                            o = (10 if d == 0 else 0) + dc
                            w = wr_v[d, 16 * b + o : 16 * b + o + 1, :]
                            term = w * src[row][b + dc]
                            total = term if total is None else total + term
                        push_v[t, g, d, 16 * b : 16 * b + 16, lanes] = total.astype(BF16)
            for d in range(2):

                @pl.when(has_x[d])
                def _():
                    x_copy(t, g, d).start()


        def receive(t, g):
            for d in range(2):

                @pl.when(has_x[d])
                def _():
                    x_copy(t, g, 1 - d).wait_recv()

            for p in range(4):
                a, b = p // 2, p % 2
                total = acc_v[g, 16 * p : 16 * p + 16, :]
                total = total + pr_v[t, g, a, 16 * b : 16 * b + 16, :].astype(F32)
                re, im = total[0:8], total[8:16]
                c = cs_v[0, p : p + 1, :]
                s = cs_v[1, p : p + 1, :]
                both = jnp.concatenate([re * c - im * s, re * s + im * c], axis=0)
                x_v[16 * p : 16 * p + 16, :] = both.astype(BF16)
            x = x_v[0:64, :]
            q0 = jnp.dot(x, radt_v[0], preferred_element_type=F32)
            q1 = jnp.dot(x, radt_v[1], preferred_element_type=F32)
            for p in range(4):
                r, i = 16 * p, 16 * p + 8
                got = jnp.concatenate(
                    [q0[r : r + 8] - q1[i : i + 8], q1[r : r + 8] + q0[i : i + 8]], axis=0
                )
                f = refl_v[p // 2, p % 2 : p % 2 + 1, :]
                new = cinc_v[g, 16 * p : 16 * p + 16, :].astype(F32) + f * got
                curf_v[g, 16 * p : 16 * p + 16, :] = new.astype(BF16)
            return curf_v[g]

        def rs_copy(n, d, peer):
            return pltpu.make_async_remote_copy(
                src_ref=sb_v.at[n, peer],
                dst_ref=rb_v.at[n, d],
                send_sem=rs_sem.at[0, n],
                recv_sem=rs_sem.at[1, n],
                device_id=x_dev(peer),
                device_id_type=MESH,
            )

        def rs_all(n):
            return pltpu.make_async_remote_copy(
                src_ref=sb_v.at[n, pl.ds(0, n_px - 1)],
                dst_ref=rb_v.at[n, pl.ds(1, n_px - 1)],
                send_sem=rs_sem.at[0, n],
                recv_sem=rs_sem.at[1, n],
                device_id=x_dev(ring(pi + 1, n_px)),
                device_id_type=MESH,
            )

        def far_field(g):
            for q in range(8):
                if q < 4:
                    total = acc_v[g, 16 * q : 16 * q + 16, :]
                else:
                    b = q % 2
                    total = push_v[1, g, (q - 4) // 2, 16 * b : 16 * b + 16, :].astype(F32)
                re, im = total[0:8], total[8:16]
                c = cs_v[0, q : q + 1, :]
                s = cs_v[1, q : q + 1, :]
                both = jnp.concatenate([re * c - im * s, re * s + im * c], axis=0)
                x_v[16 * q : 16 * q + 16, :] = both.astype(BF16)
            x = x_v[...]
            q0 = jnp.dot(x, radt_v[0], preferred_element_type=F32)
            q1 = jnp.dot(x, radt_v[1], preferred_element_type=F32)
            for q in range(8):
                r, i = 16 * q, 16 * q + 8
                got = jnp.concatenate(
                    [q0[r : r + 8] - q1[i : i + 8], q1[r : r + 8] + q0[i : i + 8]], axis=0
                )
                if q < 4:
                    new = cinc_v[g, 16 * q : 16 * q + 16, :].astype(F32)
                    new = new + refl_v[q // 2, q % 2 : q % 2 + 1, :] * got
                else:
                    new = nrefl_v[(q - 4) // 2, q % 2 : q % 2 + 1, :] * got
                xf_v[16 * q : 16 * q + 16, :] = new.astype(BF16)
            for q, (re, im) in enumerate(spectrum(xf_v[...])):
                both = jnp.concatenate([re, im], axis=0)
                x_v[16 * q : 16 * q + 16, :] = both.astype(BF16)
            x = x_v[...]
            for n in range(4):
                beams = jnp.dot(x, far_v[:, 512 * n : 512 * n + 512], preferred_element_type=F32)
                for m in range(4):
                    u = 4 * n + m
                    at = slice(LN * m, LN * m + LN)
                    far_re = far_im = None
                    for p in range(8):
                        br = beams[16 * p : 16 * p + 8, at]
                        bi = beams[16 * p + 8 : 16 * p + 16, at]
                        c = cv_v[0, p : p + 1, LN * u : LN * u + LN]
                        s = cv_v[1, p : p + 1, LN * u : LN * u + LN]
                        tr = br * c - bi * s
                        ti = br * s + bi * c
                        far_re = tr if far_re is None else far_re + tr
                        far_im = ti if far_im is None else far_im + ti
                    u_v[0, u] = far_re
                    u_v[1, u] = far_im
            spec = fft([(u_v[0, u], u_v[1, u]) for u in range(TW)])
            for t in range(0, TW, 2):
                parts = []
                for tt in (t, t + 1):
                    re, im = spec[tt]
                    if tt:
                        c = tw_v[0, tt : tt + 1, :]
                        s = tw_v[1, tt : tt + 1, :]
                        re, im = re * c + im * s, im * c - re * s
                    parts.append((re, im))
                for part in range(2):
                    y_v[8 * t : 8 * t + 16, LN * part : LN * part + LN] = jnp.concatenate(
                        [parts[0][part], parts[1][part]], axis=0
                    ).astype(BF16)
            bins = lax.dot_general(
                fm_v[...], y_v[...], (((1,), (1,)), ((), ())), preferred_element_type=F32
            )
            sb_v[g] = bins.reshape(n_px, rows_p, LN).astype(BF16)
            for d in range(1, n_px):
                peer = pi + d
                peer = jnp.where(peer >= n_px, peer - n_px, peer)
                rs_copy(g, d, peer).start()

        def z_sum_copy(g, owner):
            return pltpu.make_async_remote_copy(
                src_ref=zs_v.at[g],
                dst_ref=zb_v.at[ring(zi - owner, n_z)],
                send_sem=zs_sem.at[0],
                recv_sem=zs_sem.at[1],
                device_id=z_dev(owner),
                device_id_type=MESH,
            )

        def gather_bins(g):
            rs_all(g).wait_recv()
            total = sb_v[g, pi].astype(F32)
            for d in range(1, n_px):
                total = total + rb_v[g, d].astype(F32)
            zs_v[g] = total.astype(BF16)
            for h in range(hz):
                owner = hz * g + h

                @pl.when(zi != owner)
                def _():
                    z_sum_copy(g, owner).start()

        i_part.wait()
        i_cnt.wait()
        i_pw.wait()
        for a in range(2):
            for b in range(2):
                ids = part_v[a, b : b + 1, :]
                row = ids // cols_total
                col = ids - row * cols_total
                dr = row - (2 * pi + a) + 1
                dc = (col - (2 * zi + b) + 2 + cols_total) % cols_total
                slot = lax.broadcasted_iota(jnp.int32, (1, SLOTS), 1)
                live = slot < cnt_v[a : a + 1, b : b + 1]
                w = jnp.where(live, pw_v[a, b : b + 1, :].astype(F32), 0.0)
                kind = dr * 5 + dc
                offsets = lax.broadcasted_iota(jnp.int32, (16, SLOTS), 0)
                table = jnp.where(offsets == kind, jnp.broadcast_to(w, (16, SLOTS)), 0.0)
                column = jnp.sum(table, axis=1, keepdims=True)
                p = 2 * a + b
                w_v[16 * p : 16 * p + 16, :] = jnp.broadcast_to(column, (16, LN))

        pl.semaphore_wait(barrier, 2 + (pi > 0).astype(jnp.int32) + (pi < n_px - 1).astype(jnp.int32))
        for d in range(2):

            @pl.when(has_x[d])
            def _():
                w_copy(d).start()

        def chunks(body):
            def step(g, carry):
                body(g)
                return carry

            lax.fori_loop(0, G, step, 0)

        chunks(lambda g: radiate(0, g, cinc_v[g]))
        for copy in ins[7:]:
            copy.start()

        def z_tell(n):
            if n < len(z_rounds):
                for side in (-z_rounds[n], z_rounds[n]):
                    pl.semaphore_signal(
                        zd_sem.at[n], inc=1, device_id=z_dev(ring(zi + side, n_z)), device_id_type=MESH
                    )

        def z_hear(n):
            if n < len(z_rounds):
                pl.semaphore_wait(zd_sem.at[n], 2)

        def x_tell(n):
            if n < len(x_rounds):
                for side in (-x_rounds[n], x_rounds[n]):
                    other = pi + side

                    @pl.when((other >= 0) & (other < n_px))
                    def _():
                        pl.semaphore_signal(
                            xd_sem.at[n], inc=1, device_id=x_dev(other), device_id_type=MESH
                        )

        def x_hear(n):
            if n < len(x_rounds):
                low = (pi - x_rounds[n] >= 0).astype(jnp.int32)
                high = (pi + x_rounds[n] < n_px).astype(jnp.int32)
                pl.semaphore_wait(xd_sem.at[n], low + high)

        z_tell(0)
        x_tell(0)

        for part in range(2):
            radt_v[part] = rad_v[part].T
        i_refl.wait()
        for d in range(2):

            @pl.when(has_x[d])
            def _():
                for copy in n_copies(d):
                    copy.start()

        i_rd.wait()
        phases(rd_v, cv_v, cen_v, 0)
        i_tw.wait()
        i_fm.wait()
        i_far.wait()
        for d in range(2):

            @pl.when(has_x[d])
            def _():
                w_copy(1 - d).wait_recv()
                for copy in n_copies(1 - d):
                    copy.wait_recv()

        phases(sd_v, cs_v, ncen_v, 4)
        phases(rd_v, cv_v, ncen_v, 4)
        x_hear(0)
        x_tell(1)
        chunks(lambda g: partner_sums(0, g))
        x_hear(1)
        x_tell(2)
        z_hear(0)
        z_tell(1)
        def first_receive(g):
            radiate(1, g, receive(0, g))

            @pl.when(g == 1)
            def _():
                x_hear(2)
                x_tell(3)

        chunks(first_receive)
        x_hear(3)
        x_tell(4)
        z_hear(1)
        z_tell(2)

        def second_bounce(g):
            partner_sums(1, g)

            @pl.when(g == 0)
            def _():
                x_hear(4)

            far_field(g)

        chunks(second_bounce)
        chunks(lambda g: receive(1, g))
        z_hear(2)
        def assemble(p, carry):
            pieces = [curf_v[g, pl.ds(pl.multiple_of(16 * p, 16), 16), :].astype(F32) for g in range(G)]
            for part in range(2):
                whole = jnp.concatenate([x[8 * part : 8 * part + 8] for x in pieces], axis=0)
                cur_o[p // 2, p % 2, part] = whole.astype(BF16)
            return carry

        lax.fori_loop(0, 4, assemble, 0)
        chunks(gather_bins)

        for t in range(2):
            for g in range(G):
                for d in range(2):
                    z_copy(t, g, d).wait_send()
        for d in range(2):

            @pl.when(has_x[d])
            def _():
                w_copy(d).wait_send()
                for copy in n_copies(d):
                    copy.wait_send()
                for t in range(2):
                    for g in range(G):
                        x_copy(t, g, d).wait_send()

        for g in range(G):
            rs_all(g).wait_send()

        all_z = pltpu.make_async_remote_copy(
            src_ref=zb_v.at[pl.ds(1, n_z - 1)],
            dst_ref=zb_v.at[pl.ds(1, n_z - 1)],
            send_sem=zs_sem.at[0],
            recv_sem=zs_sem.at[1],
            device_id=z_dev(z_nb[0]),
            device_id_type=MESH,
        )
        all_z.wait_recv()
        total = zs_v[zi // hz].astype(F32)
        for d in range(1, n_z):
            total = total + zb_v[d].astype(F32)
        power = total * total
        power = (power[0:qp] + power[qp : 2 * qp]) * scale
        if qp < 8:
            power = jnp.concatenate([power, jnp.zeros((8 - qp, LN), F32)], axis=0)
        width = TW * qp
        lane = lax.broadcasted_iota(jnp.int32, (LN, width), 0)
        bin_id = lax.broadcasted_iota(jnp.int32, (LN, width), 1)
        row_id = lax.broadcasted_iota(jnp.int32, (max(qp, 8), width), 0)
        bin_row = lax.broadcasted_iota(jnp.int32, (max(qp, 8), width), 1) // TW
        first = lax.rem(zi, hz) * kz
        for b in range(kz):
            pick = jnp.where(lane == (bin_id % TW) * KC + first + b, 1.0, 0.0)
            rows = jnp.dot(power, pick, precision=lax.Precision.HIGHEST, preferred_element_type=F32)
            img_o[b : b + 1, :] = jnp.sum(
                jnp.where(row_id == bin_row, rows, 0.0), axis=0, keepdims=True
            )
        all_z.wait_send()

    return kernel


def hand_over(cur_i, img_i, cur_o, img_o, sem):
    copies = [
        pltpu.make_async_copy(cur_i, cur_o, sem.at[0]),
        pltpu.make_async_copy(img_i, img_o, sem.at[1]),
    ]
    for copy in copies:
        copy.start()
    for copy in copies:
        copy.wait()


def tables(n_px):
    qp = LN // n_px
    row = np.arange(2 * LN)
    part_out = (row // qp) % 2
    q = (row // (2 * qp)) * qp + row % qp
    col = np.arange(2 * LN)
    part_in, v = col // LN, col % LN
    turn = (q[:, None] * v[None, :] + (LN // 4) * (part_out[:, None] - part_in[None, :])) % LN
    second = np.cos(2 * math.pi * turn / LN).astype(np.float32)
    angle = 2 * math.pi * np.arange(TW)[:, None] * np.arange(LN)[None, :] / (TW * LN)
    twiddle = np.stack([np.cos(angle), np.sin(angle)]).astype(np.float32)
    return second, twiddle


def solution(mesh):
    n_px, n_z = mesh.shape["px"], mesh.shape["py"]

    def local(cin, rad, far, refl, cen, sd, rd, part, cnt, pw):
        illum, units = cin.shape[3], cin.shape[4]
        rcv = rd.shape[1]
        dirs = sd.shape[1]
        second, twiddle = tables(n_px)
        qp = LN // n_px
        kz = illum // n_z
        kernel = make_kernel(n_px, n_z, illum, rcv)
        V = pltpu.VMEM
        dma = pltpu.SemaphoreType.DMA
        regular = pltpu.SemaphoreType.REGULAR
        scratch = [
            V(cin.shape, BF16),
            V(rad.shape, BF16),
            V((2, dirs, units), BF16),
            V(far.shape, BF16),
            V(refl.shape, F32),
            V((2, 2, 3), F32),
            V(sd.shape, F32),
            V(rd.shape, F32),
            V(part.shape, jnp.int32),
            V(cnt.shape, jnp.int32),
            V(pw.shape, BF16),
            V((2 * LN, 2 * LN), BF16),
            V((2, TW, LN), F32),
            V((64, LN), F32),
            V((2, 32, LN), F32),
            V((2, 2, units), F32),
            V((2, 2, 3), F32),
            V((2, 8, dirs), F32),
            V((2, 8, rcv), F32),
            V((G, 64, units), BF16),
            V((128, units), BF16),
            V((2, G, 64, dirs), BF16),
            V((2, G, 2, 64, dirs), BF16),
            V((G, 64, dirs), F32),
            V((2, G, 2, 32, dirs), BF16),
            V((2, G, 2, 32, dirs), BF16),
            V((G, 64, units), BF16),
            V((2, TW, KC, LN), F32),
            V((128, units), BF16),
            V((LN, 2 * LN), BF16),
            V((G, n_px, 2 * qp, LN), BF16),
            V((G, n_px, 2 * qp, LN), BF16),
            V((G, 2 * qp, LN), BF16),
            V((n_z, 2 * qp, LN), BF16),
            dma((12,)),
            dma((2, 2)),
            dma((2, 2, 2)),
            dma((2, 2, G, 2)),
            dma((2, 2, G, 2)),
            dma((2, G)),
            dma((2,)),
            regular((max(1, len(doubling(n_z // 2))),)),
            regular((max(1, len(doubling(n_px - 1))),)),
        ]
        results = pl.pallas_call(
            kernel,
            out_shape=(
                pltpu.VMEM(cin.shape, BF16),
                pltpu.VMEM((kz, TW * qp), F32),
            ),
            in_specs=[pl.BlockSpec(memory_space=pltpu.HBM)] * 12,
            out_specs=(
                pl.BlockSpec(memory_space=pltpu.VMEM),
                pl.BlockSpec(memory_space=pltpu.VMEM),
            ),
            scratch_shapes=scratch,
            compiler_params=pltpu.CompilerParams(
                collective_id=0, has_side_effects=True, vmem_limit_bytes=60 << 20
            ),
        )(
            cin, rad, far, refl, jnp.transpose(cen, (1, 2, 0)), sd, rd, part, cnt, pw,
            jnp.asarray(second, BF16), jnp.asarray(twiddle),
        )
        return pl.pallas_call(
            hand_over,
            out_shape=(
                jax.ShapeDtypeStruct(cin.shape, BF16),
                jax.ShapeDtypeStruct((kz, TW * qp), F32),
            ),
            in_specs=[pl.BlockSpec(memory_space=pl.ANY)] * 2,
            out_specs=(pl.BlockSpec(memory_space=pl.ANY), pl.BlockSpec(memory_space=pl.ANY)),
            scratch_shapes=[dma((2,))],
            compiler_params=pltpu.CompilerParams(vmem_limit_bytes=1 << 20),
        )(*results)

    in_specs = (
        P("px", "py", None, None, None),
        P(),
        P(),
        P("px", "py", None),
        P(None, "px", "py"),
        P(),
        P(),
        P("px", "py", None),
        P("px", "py"),
        P("px", "py", None),
    )
    out_specs = (P("px", "py", None, None, None), P("py", "px"))
    return jax.shard_map(local, mesh=mesh, in_specs=in_specs, out_specs=out_specs, check_vma=False)
```

```python
import math

import numpy as np

import jax
import jax.numpy as jnp
from jax import lax
from jax.experimental import pallas as pl
from jax.experimental.pallas import tpu as pltpu
from jax.sharding import PartitionSpec as P

MESH = pl.DeviceIdType.MESH
F32 = jnp.float32
BF16 = jnp.bfloat16
SLOTS = 12
G = 4
KC = 8
TW = 16
LN = 128


def fft(values):
    size = len(values)
    if size == 1:
        return values
    even = fft(values[0::2])
    odd = fft(values[1::2])
    low, high = [], []
    for t in range(size // 2):
        re, im = odd[t]
        if t == 0:
            pass
        elif 4 * t == size:
            re, im = im, -re
        else:
            c = math.cos(2 * math.pi * t / size)
            s = math.sin(2 * math.pi * t / size)
            if 8 * t == size:
                re, im = (re + im) * c, (im - re) * c
            elif 8 * t == 3 * size:
                re, im = (im - re) * s, (re + im) * (-s)
            else:
                re, im = re * c + im * s, im * c - re * s
        er, ei = even[t]
        low.append((er + re, ei + im))
        high.append((er - re, ei - im))
    return low + high


def doubling(reach):
    radii, radius = [], 1
    while radius < reach:
        radii.append(radius)
        radius *= 2
    return radii


def make_kernel(n_px, n_z, illum, rcv):
    cols_total = 2 * n_z
    patches = 4 * n_px * n_z
    qp = LN // n_px
    rows_p = 2 * qp
    kz = illum // n_z
    hz = KC // kz
    z_rounds = doubling(n_z // 2)
    x_rounds = doubling(n_px - 1)
    scale = 0.125 / (patches * rcv)

    def kernel(
        cin_h, rad_h, far_h, refl_h, cen_h, sd_h, rd_h, part_h, cnt_h, pw_h, fm_h, tw_h,
        cur_o, img_o,
        cin_v, rad_v, radt_v, far_v, refl_v, cen_v, sd_v, rd_v, part_v, cnt_v, pw_v, fm_v, tw_v,
        w_v, wr_v, nrefl_v, ncen_v, cs_v, cv_v, cinc_v, x_v, own_v, zr_v, acc_v, push_v, pr_v, curf_v,
        u_v, xf_v, y_v, sb_v, rb_v, zs_v, zb_v,
        in_sem, w_sem, n_sem, zx_sem, px_sem, rs_sem, zs_sem, zd_sem, xd_sem,
    ):
        pi = lax.axis_index("px")
        zi = lax.axis_index("py")

        def ring(value, count):
            return lax.rem(value + count, count)

        z_nb = (ring(zi - 1, n_z), ring(zi + 1, n_z))
        x_nb = (ring(pi - 1, n_px), ring(pi + 1, n_px))
        has_x = (pi > 0, pi < n_px - 1)

        def z_dev(z):
            return (pi, z)

        def x_dev(x):
            return (x, zi)

        barrier = pltpu.get_barrier_semaphore()
        for z in z_nb:
            pl.semaphore_signal(barrier, inc=1, device_id=z_dev(z), device_id_type=MESH)
        for d in range(2):

            @pl.when(has_x[d])
            def _():
                pl.semaphore_signal(barrier, inc=1, device_id=x_dev(x_nb[d]), device_id_type=MESH)


        ins = []
        for n, (src, dst) in enumerate(
            (
                (sd_h, sd_v), (cen_h, cen_v), (part_h, part_v), (cnt_h, cnt_v),
                (pw_h, pw_v), (cin_h, cin_v), (rad_h, rad_v), (refl_h, refl_v),
                (rd_h, rd_v), (tw_h, tw_v), (fm_h, fm_v), (far_h, far_v),
            )
        ):
            copy = pltpu.make_async_copy(src, dst, in_sem.at[n])
            if n < 7:
                copy.start()
            ins.append(copy)
        (i_sd, i_cen, i_part, i_cnt, i_pw, i_cin, i_rad, i_refl, i_rd, i_tw, i_fm, i_far) = ins

        def phases(dirs, out, cen, first):
            for n in range(4):
                total = None
                for d in range(3):
                    term = dirs[d : d + 1, :] * cen[n // 2, n % 2 : n % 2 + 1, d : d + 1]
                    total = term if total is None else total + term
                out[0, first + n : first + n + 1, :] = total
            phi = out[0, first : first + 4, :]
            out[0, first : first + 4, :] = jnp.cos(phi)
            out[1, first : first + 4, :] = jnp.sin(phi)

        for d in range(2):

            @pl.when(jnp.logical_not(has_x[d]))
            def _():
                wr_v[d] = jnp.zeros(wr_v.shape[1:], F32)
                nrefl_v[d] = jnp.zeros(nrefl_v.shape[1:], F32)
                ncen_v[d] = jnp.zeros(ncen_v.shape[1:], F32)
                for t in range(2):
                    for g in range(G):
                        pr_v[t, g, d] = jnp.zeros(pr_v.shape[3:], BF16)

        i_sd.wait()
        i_cen.wait()
        phases(sd_v, cs_v, cen_v, 0)

        i_cin.wait()
        for p in range(4):
            x0 = cin_v[p // 2, p % 2, 0].astype(F32)
            x1 = cin_v[p // 2, p % 2, 1].astype(F32)
            for g in range(G):
                both = jnp.concatenate([x0[KC * g : KC * g + KC], x1[KC * g : KC * g + KC]], axis=0)
                cinc_v[g, 16 * p : 16 * p + 16, :] = both.astype(BF16)
        i_rad.wait()

        def spectrum(x):
            x0 = jnp.dot(x, rad_v[0], preferred_element_type=F32)
            x1 = jnp.dot(x, rad_v[1], preferred_element_type=F32)
            out = []
            for p in range(x.shape[0] // 16):
                r, i = 16 * p, 16 * p + 8
                out.append((x0[r : r + 8] - x1[i : i + 8], x1[r : r + 8] + x0[i : i + 8]))
            return out

        def z_copy(t, g, d):
            return pltpu.make_async_remote_copy(
                src_ref=own_v.at[t, g],
                dst_ref=zr_v.at[t, g, 1 - d],
                send_sem=zx_sem.at[0, t, g, d],
                recv_sem=zx_sem.at[1, t, g, 1 - d],
                device_id=z_dev(z_nb[d]),
                device_id_type=MESH,
            )

        def x_copy(t, g, d):
            return pltpu.make_async_remote_copy(
                src_ref=push_v.at[t, g, d],
                dst_ref=pr_v.at[t, g, 1 - d],
                send_sem=px_sem.at[0, t, g, d],
                recv_sem=px_sem.at[1, t, g, 1 - d],
                device_id=x_dev(x_nb[d]),
                device_id_type=MESH,
            )

        def w_copy(d):
            return pltpu.make_async_remote_copy(
                src_ref=w_v.at[pl.ds(32 * d, 32)],
                dst_ref=wr_v.at[1 - d],
                send_sem=w_sem.at[0, d],
                recv_sem=w_sem.at[1, 1 - d],
                device_id=x_dev(x_nb[d]),
                device_id_type=MESH,
            )

        def n_copies(d):
            return [
                pltpu.make_async_remote_copy(
                    src_ref=src.at[d],
                    dst_ref=dst.at[1 - d],
                    send_sem=n_sem.at[0, n, d],
                    recv_sem=n_sem.at[1, n, 1 - d],
                    device_id=x_dev(x_nb[d]),
                    device_id_type=MESH,
                )
                for n, (src, dst) in enumerate(((refl_v, nrefl_v), (cen_v, ncen_v)))
            ]

        def radiate(t, g, x):
            for p, (re, im) in enumerate(spectrum(x)):
                c = cs_v[0, p : p + 1, :]
                s = cs_v[1, p : p + 1, :]
                both = jnp.concatenate([re * c + im * s, im * c - re * s], axis=0)
                own_v[t, g, 16 * p : 16 * p + 16, :] = both.astype(BF16)
            for d in range(2):
                z_copy(t, g, d).start()

        def partner_sums(t, g):
            for d in range(2):
                z_copy(t, g, d).wait_recv()
            for j in range(4):
                lanes = slice(128 * j, 128 * j + 128)

                def source(row, e):
                    if e < 2:
                        return zr_v[t, g, 0, 16 * (2 * row + e) : 16 * (2 * row + e) + 16, lanes]
                    if e < 4:
                        return own_v[t, g, 16 * (2 * row + e - 2) : 16 * (2 * row + e - 2) + 16, lanes]
                    return zr_v[t, g, 1, 16 * (2 * row + e - 4) : 16 * (2 * row + e - 4) + 16, lanes]

                src = [[source(row, e).astype(F32) for e in range(6)] for row in range(2)]
                for a in range(2):
                    for b in range(2):
                        p = 2 * a + b
                        total = None
                        for row in range(2):
                            for dc in range(5):
                                if row == a and dc == 2:
                                    continue
                                o = (row - a + 1) * 5 + dc
                                w = w_v[16 * p + o : 16 * p + o + 1, :]
                                term = w * src[row][b + dc]
                                total = term if total is None else total + term
                        acc_v[g, 16 * p : 16 * p + 16, lanes] = total
                for d in range(2):
                    row = d
                    for b in range(2):
                        total = None
                        for dc in range(5):
                            o = (10 if d == 0 else 0) + dc
                            w = wr_v[d, 16 * b + o : 16 * b + o + 1, :]
                            term = w * src[row][b + dc]
                            total = term if total is None else total + term
                        push_v[t, g, d, 16 * b : 16 * b + 16, lanes] = total.astype(BF16)
            for d in range(2):

                @pl.when(has_x[d])
                def _():
                    x_copy(t, g, d).start()


        def receive(t, g):
            for d in range(2):

                @pl.when(has_x[d])
                def _():
                    x_copy(t, g, 1 - d).wait_recv()

            for p in range(4):
                a, b = p // 2, p % 2
                total = acc_v[g, 16 * p : 16 * p + 16, :]
                total = total + pr_v[t, g, a, 16 * b : 16 * b + 16, :].astype(F32)
                re, im = total[0:8], total[8:16]
                c = cs_v[0, p : p + 1, :]
                s = cs_v[1, p : p + 1, :]
                both = jnp.concatenate([re * c - im * s, re * s + im * c], axis=0)
                x_v[16 * p : 16 * p + 16, :] = both.astype(BF16)
            x = x_v[0:64, :]
            q0 = jnp.dot(x, radt_v[0], preferred_element_type=F32)
            q1 = jnp.dot(x, radt_v[1], preferred_element_type=F32)
            for p in range(4):
                r, i = 16 * p, 16 * p + 8
                got = jnp.concatenate(
                    [q0[r : r + 8] - q1[i : i + 8], q1[r : r + 8] + q0[i : i + 8]], axis=0
                )
                f = refl_v[p // 2, p % 2 : p % 2 + 1, :]
                new = cinc_v[g, 16 * p : 16 * p + 16, :].astype(F32) + f * got
                curf_v[g, 16 * p : 16 * p + 16, :] = new.astype(BF16)
            return curf_v[g]

        def rs_copy(n, d, peer):
            return pltpu.make_async_remote_copy(
                src_ref=sb_v.at[n, peer],
                dst_ref=rb_v.at[n, d],
                send_sem=rs_sem.at[0, n],
                recv_sem=rs_sem.at[1, n],
                device_id=x_dev(peer),
                device_id_type=MESH,
            )

        def rs_all(n):
            return pltpu.make_async_remote_copy(
                src_ref=sb_v.at[n, pl.ds(0, n_px - 1)],
                dst_ref=rb_v.at[n, pl.ds(1, n_px - 1)],
                send_sem=rs_sem.at[0, n],
                recv_sem=rs_sem.at[1, n],
                device_id=x_dev(ring(pi + 1, n_px)),
                device_id_type=MESH,
            )

        def far_field(g):
            for q in range(8):
                if q < 4:
                    total = acc_v[g, 16 * q : 16 * q + 16, :]
                else:
                    b = q % 2
                    total = push_v[1, g, (q - 4) // 2, 16 * b : 16 * b + 16, :].astype(F32)
                re, im = total[0:8], total[8:16]
                c = cs_v[0, q : q + 1, :]
                s = cs_v[1, q : q + 1, :]
                both = jnp.concatenate([re * c - im * s, re * s + im * c], axis=0)
                x_v[16 * q : 16 * q + 16, :] = both.astype(BF16)
            x = x_v[...]
            q0 = jnp.dot(x, radt_v[0], preferred_element_type=F32)
            q1 = jnp.dot(x, radt_v[1], preferred_element_type=F32)
            for q in range(8):
                r, i = 16 * q, 16 * q + 8
                got = jnp.concatenate(
                    [q0[r : r + 8] - q1[i : i + 8], q1[r : r + 8] + q0[i : i + 8]], axis=0
                )
                if q < 4:
                    new = cinc_v[g, 16 * q : 16 * q + 16, :].astype(F32)
                    new = new + refl_v[q // 2, q % 2 : q % 2 + 1, :] * got
                else:
                    new = nrefl_v[(q - 4) // 2, q % 2 : q % 2 + 1, :] * got
                xf_v[16 * q : 16 * q + 16, :] = new.astype(BF16)
            for q, (re, im) in enumerate(spectrum(xf_v[...])):
                both = jnp.concatenate([re, im], axis=0)
                x_v[16 * q : 16 * q + 16, :] = both.astype(BF16)
            x = x_v[...]
            for n in range(4):
                beams = jnp.dot(x, far_v[:, 512 * n : 512 * n + 512], preferred_element_type=F32)
                for m in range(4):
                    u = 4 * n + m
                    at = slice(LN * m, LN * m + LN)
                    far_re = far_im = None
                    for p in range(8):
                        br = beams[16 * p : 16 * p + 8, at]
                        bi = beams[16 * p + 8 : 16 * p + 16, at]
                        c = cv_v[0, p : p + 1, LN * u : LN * u + LN]
                        s = cv_v[1, p : p + 1, LN * u : LN * u + LN]
                        tr = br * c - bi * s
                        ti = br * s + bi * c
                        far_re = tr if far_re is None else far_re + tr
                        far_im = ti if far_im is None else far_im + ti
                    u_v[0, u] = far_re
                    u_v[1, u] = far_im
            spec = fft([(u_v[0, u], u_v[1, u]) for u in range(TW)])
            for t in range(0, TW, 2):
                parts = []
                for tt in (t, t + 1):
                    re, im = spec[tt]
                    if tt:
                        c = tw_v[0, tt : tt + 1, :]
                        s = tw_v[1, tt : tt + 1, :]
                        re, im = re * c + im * s, im * c - re * s
                    parts.append((re, im))
                for part in range(2):
                    y_v[8 * t : 8 * t + 16, LN * part : LN * part + LN] = jnp.concatenate(
                        [parts[0][part], parts[1][part]], axis=0
                    ).astype(BF16)
            bins = lax.dot_general(
                fm_v[...], y_v[...], (((1,), (1,)), ((), ())), preferred_element_type=F32
            )
            sb_v[g] = bins.reshape(n_px, rows_p, LN).astype(BF16)
            for d in range(1, n_px):
                peer = pi + d
                peer = jnp.where(peer >= n_px, peer - n_px, peer)
                rs_copy(g, d, peer).start()

        def z_sum_copy(g, owner):
            return pltpu.make_async_remote_copy(
                src_ref=zs_v.at[g],
                dst_ref=zb_v.at[ring(zi - owner, n_z)],
                send_sem=zs_sem.at[0],
                recv_sem=zs_sem.at[1],
                device_id=z_dev(owner),
                device_id_type=MESH,
            )

        def gather_bins(g):
            rs_all(g).wait_recv()
            total = sb_v[g, pi].astype(F32)
            for d in range(1, n_px):
                total = total + rb_v[g, d].astype(F32)
            zs_v[g] = total.astype(BF16)
            for h in range(hz):
                owner = hz * g + h

                @pl.when(zi != owner)
                def _():
                    z_sum_copy(g, owner).start()

        i_part.wait()
        i_cnt.wait()
        i_pw.wait()
        for a in range(2):
            for b in range(2):
                ids = part_v[a, b : b + 1, :]
                row = ids // cols_total
                col = ids - row * cols_total
                dr = row - (2 * pi + a) + 1
                dc = (col - (2 * zi + b) + 2 + cols_total) % cols_total
                slot = lax.broadcasted_iota(jnp.int32, (1, SLOTS), 1)
                live = slot < cnt_v[a : a + 1, b : b + 1]
                w = jnp.where(live, pw_v[a, b : b + 1, :].astype(F32), 0.0)
                kind = dr * 5 + dc
                offsets = lax.broadcasted_iota(jnp.int32, (16, SLOTS), 0)
                table = jnp.where(offsets == kind, jnp.broadcast_to(w, (16, SLOTS)), 0.0)
                column = jnp.sum(table, axis=1, keepdims=True)
                p = 2 * a + b
                w_v[16 * p : 16 * p + 16, :] = jnp.broadcast_to(column, (16, LN))

        pl.semaphore_wait(barrier, 2 + (pi > 0).astype(jnp.int32) + (pi < n_px - 1).astype(jnp.int32))
        for d in range(2):

            @pl.when(has_x[d])
            def _():
                w_copy(d).start()

        def chunks(body, first=0, last=G):
            def step(g, carry):
                body(g)
                return carry

            lax.fori_loop(first, last, step, 0)

        chunks(lambda g: radiate(0, g, cinc_v[g]))
        for copy in ins[7:]:
            copy.start()

        def z_tell(n):
            if n < len(z_rounds):
                for side in (-z_rounds[n], z_rounds[n]):
                    pl.semaphore_signal(
                        zd_sem.at[n], inc=1, device_id=z_dev(ring(zi + side, n_z)), device_id_type=MESH
                    )

        def z_hear(n):
            if n < len(z_rounds):
                pl.semaphore_wait(zd_sem.at[n], 2)

        def x_tell(n):
            if n < len(x_rounds):
                for side in (-x_rounds[n], x_rounds[n]):
                    other = pi + side

                    @pl.when((other >= 0) & (other < n_px))
                    def _():
                        pl.semaphore_signal(
                            xd_sem.at[n], inc=1, device_id=x_dev(other), device_id_type=MESH
                        )

        def x_hear(n):
            if n < len(x_rounds):
                low = (pi - x_rounds[n] >= 0).astype(jnp.int32)
                high = (pi + x_rounds[n] < n_px).astype(jnp.int32)
                pl.semaphore_wait(xd_sem.at[n], low + high)

        z_tell(0)
        x_tell(0)

        for part in range(2):
            radt_v[part] = rad_v[part].T
        i_refl.wait()
        for d in range(2):

            @pl.when(has_x[d])
            def _():
                for copy in n_copies(d):
                    copy.start()

        i_rd.wait()
        phases(rd_v, cv_v, cen_v, 0)
        i_tw.wait()
        i_fm.wait()
        i_far.wait()
        for d in range(2):

            @pl.when(has_x[d])
            def _():
                w_copy(1 - d).wait_recv()
                for copy in n_copies(1 - d):
                    copy.wait_recv()

        phases(sd_v, cs_v, ncen_v, 4)
        phases(rd_v, cv_v, ncen_v, 4)
        x_hear(0)
        x_tell(1)
        chunks(lambda g: partner_sums(0, g))
        x_hear(1)
        x_tell(2)
        z_hear(0)
        z_tell(1)
        def first_receive(g):
            radiate(1, g, receive(0, g))

            @pl.when(g == 1)
            def _():
                x_hear(2)
                x_tell(3)

        chunks(first_receive)
        x_hear(3)
        x_tell(4)
        z_hear(1)
        z_tell(2)

        def second_bounce(g):
            partner_sums(1, g)

            @pl.when(g == 0)
            def _():
                x_hear(4)

            far_field(g)

        chunks(second_bounce)
        chunks(lambda g: receive(1, g), 0, G // 2)
        z_hear(2)
        gather_bins(0)
        chunks(lambda g: receive(1, g), G // 2, G)
        def assemble(p, carry):
            pieces = [curf_v[g, pl.ds(pl.multiple_of(16 * p, 16), 16), :].astype(F32) for g in range(G)]
            for part in range(2):
                whole = jnp.concatenate([x[8 * part : 8 * part + 8] for x in pieces], axis=0)
                cur_o[p // 2, p % 2, part] = whole.astype(BF16)
            return carry

        lax.fori_loop(0, 4, assemble, 0)
        chunks(gather_bins, 1, G)

        for t in range(2):
            for g in range(G):
                for d in range(2):
                    z_copy(t, g, d).wait_send()
        for d in range(2):

            @pl.when(has_x[d])
            def _():
                w_copy(d).wait_send()
                for copy in n_copies(d):
                    copy.wait_send()
                for t in range(2):
                    for g in range(G):
                        x_copy(t, g, d).wait_send()

        for g in range(G):
            rs_all(g).wait_send()

        all_z = pltpu.make_async_remote_copy(
            src_ref=zb_v.at[pl.ds(1, n_z - 1)],
            dst_ref=zb_v.at[pl.ds(1, n_z - 1)],
            send_sem=zs_sem.at[0],
            recv_sem=zs_sem.at[1],
            device_id=z_dev(z_nb[0]),
            device_id_type=MESH,
        )
        all_z.wait_recv()
        total = zs_v[zi // hz].astype(F32)
        for d in range(1, n_z):
            total = total + zb_v[d].astype(F32)
        power = total * total
        power = (power[0:qp] + power[qp : 2 * qp]) * scale
        if qp < 8:
            power = jnp.concatenate([power, jnp.zeros((8 - qp, LN), F32)], axis=0)
        width = TW * qp
        lane = lax.broadcasted_iota(jnp.int32, (LN, width), 0)
        bin_id = lax.broadcasted_iota(jnp.int32, (LN, width), 1)
        row_id = lax.broadcasted_iota(jnp.int32, (max(qp, 8), width), 0)
        bin_row = lax.broadcasted_iota(jnp.int32, (max(qp, 8), width), 1) // TW
        first = lax.rem(zi, hz) * kz
        for b in range(kz):
            pick = jnp.where(lane == (bin_id % TW) * KC + first + b, 1.0, 0.0)
            rows = jnp.dot(power, pick, precision=lax.Precision.HIGHEST, preferred_element_type=F32)
            img_o[b : b + 1, :] = jnp.sum(
                jnp.where(row_id == bin_row, rows, 0.0), axis=0, keepdims=True
            )
        all_z.wait_send()

    return kernel


def hand_over(cur_i, img_i, cur_o, img_o, sem):
    copies = [
        pltpu.make_async_copy(cur_i, cur_o, sem.at[0]),
        pltpu.make_async_copy(img_i, img_o, sem.at[1]),
    ]
    for copy in copies:
        copy.start()
    for copy in copies:
        copy.wait()


def tables(n_px):
    qp = LN // n_px
    row = np.arange(2 * LN)
    part_out = (row // qp) % 2
    q = (row // (2 * qp)) * qp + row % qp
    col = np.arange(2 * LN)
    part_in, v = col // LN, col % LN
    turn = (q[:, None] * v[None, :] + (LN // 4) * (part_out[:, None] - part_in[None, :])) % LN
    second = np.cos(2 * math.pi * turn / LN).astype(np.float32)
    angle = 2 * math.pi * np.arange(TW)[:, None] * np.arange(LN)[None, :] / (TW * LN)
    twiddle = np.stack([np.cos(angle), np.sin(angle)]).astype(np.float32)
    return second, twiddle


def solution(mesh):
    n_px, n_z = mesh.shape["px"], mesh.shape["py"]

    def local(cin, rad, far, refl, cen, sd, rd, part, cnt, pw):
        illum, units = cin.shape[3], cin.shape[4]
        rcv = rd.shape[1]
        dirs = sd.shape[1]
        second, twiddle = tables(n_px)
        qp = LN // n_px
        kz = illum // n_z
        kernel = make_kernel(n_px, n_z, illum, rcv)
        V = pltpu.VMEM
        dma = pltpu.SemaphoreType.DMA
        regular = pltpu.SemaphoreType.REGULAR
        scratch = [
            V(cin.shape, BF16),
            V(rad.shape, BF16),
            V((2, dirs, units), BF16),
            V(far.shape, BF16),
            V(refl.shape, F32),
            V((2, 2, 3), F32),
            V(sd.shape, F32),
            V(rd.shape, F32),
            V(part.shape, jnp.int32),
            V(cnt.shape, jnp.int32),
            V(pw.shape, BF16),
            V((2 * LN, 2 * LN), BF16),
            V((2, TW, LN), F32),
            V((64, LN), F32),
            V((2, 32, LN), F32),
            V((2, 2, units), F32),
            V((2, 2, 3), F32),
            V((2, 8, dirs), F32),
            V((2, 8, rcv), F32),
            V((G, 64, units), BF16),
            V((128, units), BF16),
            V((2, G, 64, dirs), BF16),
            V((2, G, 2, 64, dirs), BF16),
            V((G, 64, dirs), F32),
            V((2, G, 2, 32, dirs), BF16),
            V((2, G, 2, 32, dirs), BF16),
            V((G, 64, units), BF16),
            V((2, TW, KC, LN), F32),
            V((128, units), BF16),
            V((LN, 2 * LN), BF16),
            V((G, n_px, 2 * qp, LN), BF16),
            V((G, n_px, 2 * qp, LN), BF16),
            V((G, 2 * qp, LN), BF16),
            V((n_z, 2 * qp, LN), BF16),
            dma((12,)),
            dma((2, 2)),
            dma((2, 2, 2)),
            dma((2, 2, G, 2)),
            dma((2, 2, G, 2)),
            dma((2, G)),
            dma((2,)),
            regular((max(1, len(doubling(n_z // 2))),)),
            regular((max(1, len(doubling(n_px - 1))),)),
        ]
        results = pl.pallas_call(
            kernel,
            out_shape=(
                pltpu.VMEM(cin.shape, BF16),
                pltpu.VMEM((kz, TW * qp), F32),
            ),
            in_specs=[pl.BlockSpec(memory_space=pltpu.HBM)] * 12,
            out_specs=(
                pl.BlockSpec(memory_space=pltpu.VMEM),
                pl.BlockSpec(memory_space=pltpu.VMEM),
            ),
            scratch_shapes=scratch,
            compiler_params=pltpu.CompilerParams(
                collective_id=0, has_side_effects=True, vmem_limit_bytes=60 << 20
            ),
        )(
            cin, rad, far, refl, jnp.transpose(cen, (1, 2, 0)), sd, rd, part, cnt, pw,
            jnp.asarray(second, BF16), jnp.asarray(twiddle),
        )
        return pl.pallas_call(
            hand_over,
            out_shape=(
                jax.ShapeDtypeStruct(cin.shape, BF16),
                jax.ShapeDtypeStruct((kz, TW * qp), F32),
            ),
            in_specs=[pl.BlockSpec(memory_space=pl.ANY)] * 2,
            out_specs=(pl.BlockSpec(memory_space=pl.ANY), pl.BlockSpec(memory_space=pl.ANY)),
            scratch_shapes=[dma((2,))],
            compiler_params=pltpu.CompilerParams(vmem_limit_bytes=1 << 20),
        )(*results)

    in_specs = (
        P("px", "py", None, None, None),
        P(),
        P(),
        P("px", "py", None),
        P(None, "px", "py"),
        P(),
        P(),
        P("px", "py", None),
        P("px", "py"),
        P("px", "py", None),
    )
    out_specs = (P("px", "py", None, None, None), P("py", "px"))
    return jax.shard_map(local, mesh=mesh, in_specs=in_specs, out_specs=out_specs, check_vma=False)
```

```python
import math

import numpy as np

import jax
import jax.numpy as jnp
from jax import lax
from jax.experimental import pallas as pl
from jax.experimental.pallas import tpu as pltpu
from jax.sharding import PartitionSpec as P

MESH = pl.DeviceIdType.MESH
F32 = jnp.float32
BF16 = jnp.bfloat16
SLOTS = 12
G = 4
KC = 8
TW = 16
LN = 128


def fft(values):
    size = len(values)
    if size == 1:
        return values
    even = fft(values[0::2])
    odd = fft(values[1::2])
    low, high = [], []
    for t in range(size // 2):
        re, im = odd[t]
        if t == 0:
            pass
        elif 4 * t == size:
            re, im = im, -re
        else:
            c = math.cos(2 * math.pi * t / size)
            s = math.sin(2 * math.pi * t / size)
            if 8 * t == size:
                re, im = (re + im) * c, (im - re) * c
            elif 8 * t == 3 * size:
                re, im = (im - re) * s, (re + im) * (-s)
            else:
                re, im = re * c + im * s, im * c - re * s
        er, ei = even[t]
        low.append((er + re, ei + im))
        high.append((er - re, ei - im))
    return low + high


def doubling(reach):
    radii, radius = [], 1
    while radius < reach:
        radii.append(radius)
        radius *= 2
    return radii


def make_kernel(n_px, n_z, illum, rcv):
    cols_total = 2 * n_z
    patches = 4 * n_px * n_z
    qp = LN // n_px
    rows_p = 2 * qp
    kz = illum // n_z
    hz = KC // kz
    z_rounds = doubling(n_z // 2)
    x_rounds = doubling(n_px - 1)
    scale = 0.125 / (patches * rcv)

    def kernel(
        cin_h, rad_h, far_h, refl_h, cen_h, sd_h, rd_h, part_h, cnt_h, pw_h, fm_h, tw_h,
        cur_o, img_o,
        cin_v, rad_v, radt_v, far_v, refl_v, cen_v, sd_v, rd_v, part_v, cnt_v, pw_v, fm_v, tw_v,
        w_v, wr_v, nrefl_v, ncen_v, cs_v, cv_v, cinc_v, x_v, own_v, zr_v, acc_v, push_v, pr_v, curf_v,
        u_v, xf_v, y_v, sb_v, rb_v, zs_v, zb_v,
        in_sem, w_sem, n_sem, zx_sem, px_sem, rs_sem, zs_sem, zd_sem, xd_sem,
    ):
        pi = lax.axis_index("px")
        zi = lax.axis_index("py")

        def ring(value, count):
            return lax.rem(value + count, count)

        z_nb = (ring(zi - 1, n_z), ring(zi + 1, n_z))
        x_nb = (ring(pi - 1, n_px), ring(pi + 1, n_px))
        has_x = (pi > 0, pi < n_px - 1)

        def z_dev(z):
            return (pi, z)

        def x_dev(x):
            return (x, zi)

        barrier = pltpu.get_barrier_semaphore()
        for z in z_nb:
            pl.semaphore_signal(barrier, inc=1, device_id=z_dev(z), device_id_type=MESH)
        for d in range(2):

            @pl.when(has_x[d])
            def _():
                pl.semaphore_signal(barrier, inc=1, device_id=x_dev(x_nb[d]), device_id_type=MESH)


        ins = []
        for n, (src, dst) in enumerate(
            (
                (sd_h, sd_v), (cen_h, cen_v), (part_h, part_v), (cnt_h, cnt_v),
                (pw_h, pw_v), (cin_h, cin_v), (rad_h, rad_v), (refl_h, refl_v),
                (rd_h, rd_v), (tw_h, tw_v), (fm_h, fm_v), (far_h, far_v),
            )
        ):
            copy = pltpu.make_async_copy(src, dst, in_sem.at[n])
            if n < 7:
                copy.start()
            ins.append(copy)
        (i_sd, i_cen, i_part, i_cnt, i_pw, i_cin, i_rad, i_refl, i_rd, i_tw, i_fm, i_far) = ins

        def phases(dirs, out, cen, first):
            for n in range(4):
                total = None
                for d in range(3):
                    term = dirs[d : d + 1, :] * cen[n // 2, n % 2 : n % 2 + 1, d : d + 1]
                    total = term if total is None else total + term
                out[0, first + n : first + n + 1, :] = total
            phi = out[0, first : first + 4, :]
            out[0, first : first + 4, :] = jnp.cos(phi)
            out[1, first : first + 4, :] = jnp.sin(phi)

        for d in range(2):

            @pl.when(jnp.logical_not(has_x[d]))
            def _():
                wr_v[d] = jnp.zeros(wr_v.shape[1:], F32)
                nrefl_v[d] = jnp.zeros(nrefl_v.shape[1:], F32)
                ncen_v[d] = jnp.zeros(ncen_v.shape[1:], F32)
                for t in range(2):
                    for g in range(G):
                        pr_v[t, g, d] = jnp.zeros(pr_v.shape[3:], BF16)

        i_sd.wait()
        i_cen.wait()
        phases(sd_v, cs_v, cen_v, 0)

        i_cin.wait()
        for p in range(4):
            x0 = cin_v[p // 2, p % 2, 0].astype(F32)
            x1 = cin_v[p // 2, p % 2, 1].astype(F32)
            for g in range(G):
                both = jnp.concatenate([x0[KC * g : KC * g + KC], x1[KC * g : KC * g + KC]], axis=0)
                cinc_v[g, 16 * p : 16 * p + 16, :] = both.astype(BF16)
        i_rad.wait()

        def spectrum(x):
            x0 = jnp.dot(x, rad_v[0], preferred_element_type=F32)
            x1 = jnp.dot(x, rad_v[1], preferred_element_type=F32)
            out = []
            for p in range(x.shape[0] // 16):
                r, i = 16 * p, 16 * p + 8
                out.append((x0[r : r + 8] - x1[i : i + 8], x1[r : r + 8] + x0[i : i + 8]))
            return out

        def z_copy(t, g, d):
            return pltpu.make_async_remote_copy(
                src_ref=own_v.at[t, g],
                dst_ref=zr_v.at[t, g, 1 - d],
                send_sem=zx_sem.at[0, t, g, d],
                recv_sem=zx_sem.at[1, t, g, 1 - d],
                device_id=z_dev(z_nb[d]),
                device_id_type=MESH,
            )

        def x_copy(t, g, d):
            return pltpu.make_async_remote_copy(
                src_ref=push_v.at[t, g, d],
                dst_ref=pr_v.at[t, g, 1 - d],
                send_sem=px_sem.at[0, t, g, d],
                recv_sem=px_sem.at[1, t, g, 1 - d],
                device_id=x_dev(x_nb[d]),
                device_id_type=MESH,
            )

        def w_copy(d):
            return pltpu.make_async_remote_copy(
                src_ref=w_v.at[pl.ds(32 * d, 32)],
                dst_ref=wr_v.at[1 - d],
                send_sem=w_sem.at[0, d],
                recv_sem=w_sem.at[1, 1 - d],
                device_id=x_dev(x_nb[d]),
                device_id_type=MESH,
            )

        def n_copies(d):
            return [
                pltpu.make_async_remote_copy(
                    src_ref=src.at[d],
                    dst_ref=dst.at[1 - d],
                    send_sem=n_sem.at[0, n, d],
                    recv_sem=n_sem.at[1, n, 1 - d],
                    device_id=x_dev(x_nb[d]),
                    device_id_type=MESH,
                )
                for n, (src, dst) in enumerate(((refl_v, nrefl_v), (cen_v, ncen_v)))
            ]

        def radiate(t, g, x):
            for p, (re, im) in enumerate(spectrum(x)):
                c = cs_v[0, p : p + 1, :]
                s = cs_v[1, p : p + 1, :]
                both = jnp.concatenate([re * c + im * s, im * c - re * s], axis=0)
                own_v[t, g, 16 * p : 16 * p + 16, :] = both.astype(BF16)
            for d in range(2):
                z_copy(t, g, d).start()

        def partner_sums(t, g):
            for d in range(2):
                z_copy(t, g, d).wait_recv()
            for j in range(4):
                lanes = slice(128 * j, 128 * j + 128)

                def source(row, e):
                    if e < 2:
                        return zr_v[t, g, 0, 16 * (2 * row + e) : 16 * (2 * row + e) + 16, lanes]
                    if e < 4:
                        return own_v[t, g, 16 * (2 * row + e - 2) : 16 * (2 * row + e - 2) + 16, lanes]
                    return zr_v[t, g, 1, 16 * (2 * row + e - 4) : 16 * (2 * row + e - 4) + 16, lanes]

                src = [[source(row, e).astype(F32) for e in range(6)] for row in range(2)]
                for a in range(2):
                    for b in range(2):
                        p = 2 * a + b
                        total = None
                        for row in range(2):
                            for dc in range(5):
                                if row == a and dc == 2:
                                    continue
                                o = (row - a + 1) * 5 + dc
                                w = w_v[16 * p + o : 16 * p + o + 1, :]
                                term = w * src[row][b + dc]
                                total = term if total is None else total + term
                        acc_v[g, 16 * p : 16 * p + 16, lanes] = total
                for d in range(2):
                    row = d
                    for b in range(2):
                        total = None
                        for dc in range(5):
                            o = (10 if d == 0 else 0) + dc
                            w = wr_v[d, 16 * b + o : 16 * b + o + 1, :]
                            term = w * src[row][b + dc]
                            total = term if total is None else total + term
                        push_v[t, g, d, 16 * b : 16 * b + 16, lanes] = total.astype(BF16)
            for d in range(2):

                @pl.when(has_x[d])
                def _():
                    x_copy(t, g, d).start()


        def receive(t, g):
            for d in range(2):

                @pl.when(has_x[d])
                def _():
                    x_copy(t, g, 1 - d).wait_recv()

            for p in range(4):
                a, b = p // 2, p % 2
                total = acc_v[g, 16 * p : 16 * p + 16, :]
                total = total + pr_v[t, g, a, 16 * b : 16 * b + 16, :].astype(F32)
                re, im = total[0:8], total[8:16]
                c = cs_v[0, p : p + 1, :]
                s = cs_v[1, p : p + 1, :]
                both = jnp.concatenate([re * c - im * s, re * s + im * c], axis=0)
                x_v[16 * p : 16 * p + 16, :] = both.astype(BF16)
            x = x_v[0:64, :]
            q0 = jnp.dot(x, radt_v[0], preferred_element_type=F32)
            q1 = jnp.dot(x, radt_v[1], preferred_element_type=F32)
            for p in range(4):
                r, i = 16 * p, 16 * p + 8
                got = jnp.concatenate(
                    [q0[r : r + 8] - q1[i : i + 8], q1[r : r + 8] + q0[i : i + 8]], axis=0
                )
                f = refl_v[p // 2, p % 2 : p % 2 + 1, :]
                new = cinc_v[g, 16 * p : 16 * p + 16, :].astype(F32) + f * got
                curf_v[g, 16 * p : 16 * p + 16, :] = new.astype(BF16)
            return curf_v[g]

        def rs_copy(n, d, peer):
            return pltpu.make_async_remote_copy(
                src_ref=sb_v.at[n, peer],
                dst_ref=rb_v.at[n, d],
                send_sem=rs_sem.at[0, n],
                recv_sem=rs_sem.at[1, n],
                device_id=x_dev(peer),
                device_id_type=MESH,
            )

        def rs_all(n):
            return pltpu.make_async_remote_copy(
                src_ref=sb_v.at[n, pl.ds(0, n_px - 1)],
                dst_ref=rb_v.at[n, pl.ds(1, n_px - 1)],
                send_sem=rs_sem.at[0, n],
                recv_sem=rs_sem.at[1, n],
                device_id=x_dev(ring(pi + 1, n_px)),
                device_id_type=MESH,
            )

        def far_field(g):
            for q in range(8):
                if q < 4:
                    total = acc_v[g, 16 * q : 16 * q + 16, :]
                else:
                    b = q % 2
                    total = push_v[1, g, (q - 4) // 2, 16 * b : 16 * b + 16, :].astype(F32)
                re, im = total[0:8], total[8:16]
                c = cs_v[0, q : q + 1, :]
                s = cs_v[1, q : q + 1, :]
                both = jnp.concatenate([re * c - im * s, re * s + im * c], axis=0)
                x_v[16 * q : 16 * q + 16, :] = both.astype(BF16)
            x = x_v[...]
            q0 = jnp.dot(x, radt_v[0], preferred_element_type=F32)
            q1 = jnp.dot(x, radt_v[1], preferred_element_type=F32)
            for q in range(8):
                r, i = 16 * q, 16 * q + 8
                got = jnp.concatenate(
                    [q0[r : r + 8] - q1[i : i + 8], q1[r : r + 8] + q0[i : i + 8]], axis=0
                )
                if q < 4:
                    new = cinc_v[g, 16 * q : 16 * q + 16, :].astype(F32)
                    new = new + refl_v[q // 2, q % 2 : q % 2 + 1, :] * got
                else:
                    new = nrefl_v[(q - 4) // 2, q % 2 : q % 2 + 1, :] * got
                xf_v[16 * q : 16 * q + 16, :] = new.astype(BF16)
            for q, (re, im) in enumerate(spectrum(xf_v[...])):
                both = jnp.concatenate([re, im], axis=0)
                x_v[16 * q : 16 * q + 16, :] = both.astype(BF16)
            x = x_v[...]
            for n in range(4):
                beams = jnp.dot(x, far_v[:, 512 * n : 512 * n + 512], preferred_element_type=F32)
                for m in range(4):
                    u = 4 * n + m
                    at = slice(LN * m, LN * m + LN)
                    far_re = far_im = None
                    for p in range(8):
                        br = beams[16 * p : 16 * p + 8, at]
                        bi = beams[16 * p + 8 : 16 * p + 16, at]
                        c = cv_v[0, p : p + 1, LN * u : LN * u + LN]
                        s = cv_v[1, p : p + 1, LN * u : LN * u + LN]
                        tr = br * c - bi * s
                        ti = br * s + bi * c
                        far_re = tr if far_re is None else far_re + tr
                        far_im = ti if far_im is None else far_im + ti
                    u_v[0, u] = far_re
                    u_v[1, u] = far_im
            spec = fft([(u_v[0, u], u_v[1, u]) for u in range(TW)])
            for t in range(0, TW, 2):
                parts = []
                for tt in (t, t + 1):
                    re, im = spec[tt]
                    if tt:
                        c = tw_v[0, tt : tt + 1, :]
                        s = tw_v[1, tt : tt + 1, :]
                        re, im = re * c + im * s, im * c - re * s
                    parts.append((re, im))
                for part in range(2):
                    y_v[8 * t : 8 * t + 16, LN * part : LN * part + LN] = jnp.concatenate(
                        [parts[0][part], parts[1][part]], axis=0
                    ).astype(BF16)
            bins = lax.dot_general(
                fm_v[...], y_v[...], (((1,), (1,)), ((), ())), preferred_element_type=F32
            )
            sb_v[g] = bins.reshape(n_px, rows_p, LN).astype(BF16)
            for d in range(1, n_px):
                peer = pi + d
                peer = jnp.where(peer >= n_px, peer - n_px, peer)
                rs_copy(g, d, peer).start()

        def z_sum_copy(g, owner):
            return pltpu.make_async_remote_copy(
                src_ref=zs_v.at[g],
                dst_ref=zb_v.at[ring(zi - owner, n_z)],
                send_sem=zs_sem.at[0],
                recv_sem=zs_sem.at[1],
                device_id=z_dev(owner),
                device_id_type=MESH,
            )

        def gather_bins(g):
            rs_all(g).wait_recv()
            total = sb_v[g, pi].astype(F32)
            for d in range(1, n_px):
                total = total + rb_v[g, d].astype(F32)
            zs_v[g] = total.astype(BF16)
            for h in range(hz):
                owner = hz * g + h

                @pl.when(zi != owner)
                def _():
                    z_sum_copy(g, owner).start()

        i_part.wait()
        i_cnt.wait()
        i_pw.wait()
        for a in range(2):
            for b in range(2):
                ids = part_v[a, b : b + 1, :]
                row = ids // cols_total
                col = ids - row * cols_total
                dr = row - (2 * pi + a) + 1
                dc = (col - (2 * zi + b) + 2 + cols_total) % cols_total
                slot = lax.broadcasted_iota(jnp.int32, (1, SLOTS), 1)
                live = slot < cnt_v[a : a + 1, b : b + 1]
                w = jnp.where(live, pw_v[a, b : b + 1, :].astype(F32), 0.0)
                kind = dr * 5 + dc
                offsets = lax.broadcasted_iota(jnp.int32, (16, SLOTS), 0)
                table = jnp.where(offsets == kind, jnp.broadcast_to(w, (16, SLOTS)), 0.0)
                column = jnp.sum(table, axis=1, keepdims=True)
                p = 2 * a + b
                w_v[16 * p : 16 * p + 16, :] = jnp.broadcast_to(column, (16, LN))

        pl.semaphore_wait(barrier, 2 + (pi > 0).astype(jnp.int32) + (pi < n_px - 1).astype(jnp.int32))
        for d in range(2):

            @pl.when(has_x[d])
            def _():
                w_copy(d).start()

        def chunks(body, first=0, last=G):
            def step(g, carry):
                body(g)
                return carry

            lax.fori_loop(first, last, step, 0)

        chunks(lambda g: radiate(0, g, cinc_v[g]))
        for copy in ins[7:]:
            copy.start()

        def z_tell(n):
            if n < len(z_rounds):
                for side in (-z_rounds[n], z_rounds[n]):
                    pl.semaphore_signal(
                        zd_sem.at[n], inc=1, device_id=z_dev(ring(zi + side, n_z)), device_id_type=MESH
                    )

        def z_hear(n):
            if n < len(z_rounds):
                pl.semaphore_wait(zd_sem.at[n], 2)

        def x_tell(n):
            if n < len(x_rounds):
                for side in (-x_rounds[n], x_rounds[n]):
                    other = pi + side

                    @pl.when((other >= 0) & (other < n_px))
                    def _():
                        pl.semaphore_signal(
                            xd_sem.at[n], inc=1, device_id=x_dev(other), device_id_type=MESH
                        )

        def x_hear(n):
            if n < len(x_rounds):
                low = (pi - x_rounds[n] >= 0).astype(jnp.int32)
                high = (pi + x_rounds[n] < n_px).astype(jnp.int32)
                pl.semaphore_wait(xd_sem.at[n], low + high)

        z_tell(0)
        x_tell(0)

        for part in range(2):
            radt_v[part] = rad_v[part].T
        i_refl.wait()
        for d in range(2):

            @pl.when(has_x[d])
            def _():
                for copy in n_copies(d):
                    copy.start()

        i_rd.wait()
        phases(rd_v, cv_v, cen_v, 0)
        i_tw.wait()
        i_fm.wait()
        i_far.wait()
        for d in range(2):

            @pl.when(has_x[d])
            def _():
                w_copy(1 - d).wait_recv()
                for copy in n_copies(1 - d):
                    copy.wait_recv()

        phases(sd_v, cs_v, ncen_v, 4)
        phases(rd_v, cv_v, ncen_v, 4)
        x_hear(0)
        x_tell(1)
        chunks(lambda g: partner_sums(0, g))
        x_hear(1)
        x_tell(2)
        z_hear(0)
        z_tell(1)
        def first_receive(g):
            radiate(1, g, receive(0, g))

            @pl.when(g == 1)
            def _():
                x_hear(2)
                x_tell(3)

        chunks(first_receive)
        x_hear(3)
        x_tell(4)
        z_hear(1)
        z_tell(2)

        def second_bounce(g):
            partner_sums(1, g)

            @pl.when(g == 0)
            def _():
                x_hear(4)

            far_field(g)

        chunks(second_bounce)
        chunks(lambda g: receive(1, g), 0, G // 2)
        z_hear(2)
        gather_bins(0)
        chunks(lambda g: receive(1, g), G // 2, G)
        gather_bins(1)
        def assemble(p, carry):
            pieces = [curf_v[g, pl.ds(pl.multiple_of(16 * p, 16), 16), :].astype(F32) for g in range(G)]
            for part in range(2):
                whole = jnp.concatenate([x[8 * part : 8 * part + 8] for x in pieces], axis=0)
                cur_o[p // 2, p % 2, part] = whole.astype(BF16)
            return carry

        lax.fori_loop(0, 4, assemble, 0)
        chunks(gather_bins, 2, G)

        for t in range(2):
            for g in range(G):
                for d in range(2):
                    z_copy(t, g, d).wait_send()
        for d in range(2):

            @pl.when(has_x[d])
            def _():
                w_copy(d).wait_send()
                for copy in n_copies(d):
                    copy.wait_send()
                for t in range(2):
                    for g in range(G):
                        x_copy(t, g, d).wait_send()

        for g in range(G):
            rs_all(g).wait_send()

        all_z = pltpu.make_async_remote_copy(
            src_ref=zb_v.at[pl.ds(1, n_z - 1)],
            dst_ref=zb_v.at[pl.ds(1, n_z - 1)],
            send_sem=zs_sem.at[0],
            recv_sem=zs_sem.at[1],
            device_id=z_dev(z_nb[0]),
            device_id_type=MESH,
        )
        all_z.wait_recv()
        total = zs_v[zi // hz].astype(F32)
        for d in range(1, n_z):
            total = total + zb_v[d].astype(F32)
        power = total * total
        power = (power[0:qp] + power[qp : 2 * qp]) * scale
        if qp < 8:
            power = jnp.concatenate([power, jnp.zeros((8 - qp, LN), F32)], axis=0)
        width = TW * qp
        lane = lax.broadcasted_iota(jnp.int32, (LN, width), 0)
        bin_id = lax.broadcasted_iota(jnp.int32, (LN, width), 1)
        row_id = lax.broadcasted_iota(jnp.int32, (max(qp, 8), width), 0)
        bin_row = lax.broadcasted_iota(jnp.int32, (max(qp, 8), width), 1) // TW
        first = lax.rem(zi, hz) * kz
        for b in range(kz):
            pick = jnp.where(lane == (bin_id % TW) * KC + first + b, 1.0, 0.0)
            rows = jnp.dot(power, pick, precision=lax.Precision.HIGHEST, preferred_element_type=F32)
            img_o[b : b + 1, :] = jnp.sum(
                jnp.where(row_id == bin_row, rows, 0.0), axis=0, keepdims=True
            )
        all_z.wait_send()

    return kernel


def hand_over(cur_i, img_i, cur_o, img_o, sem):
    copies = [
        pltpu.make_async_copy(cur_i, cur_o, sem.at[0]),
        pltpu.make_async_copy(img_i, img_o, sem.at[1]),
    ]
    for copy in copies:
        copy.start()
    for copy in copies:
        copy.wait()


def tables(n_px):
    qp = LN // n_px
    row = np.arange(2 * LN)
    part_out = (row // qp) % 2
    q = (row // (2 * qp)) * qp + row % qp
    col = np.arange(2 * LN)
    part_in, v = col // LN, col % LN
    turn = (q[:, None] * v[None, :] + (LN // 4) * (part_out[:, None] - part_in[None, :])) % LN
    second = np.cos(2 * math.pi * turn / LN).astype(np.float32)
    angle = 2 * math.pi * np.arange(TW)[:, None] * np.arange(LN)[None, :] / (TW * LN)
    twiddle = np.stack([np.cos(angle), np.sin(angle)]).astype(np.float32)
    return second, twiddle


def solution(mesh):
    n_px, n_z = mesh.shape["px"], mesh.shape["py"]

    def local(cin, rad, far, refl, cen, sd, rd, part, cnt, pw):
        illum, units = cin.shape[3], cin.shape[4]
        rcv = rd.shape[1]
        dirs = sd.shape[1]
        second, twiddle = tables(n_px)
        qp = LN // n_px
        kz = illum // n_z
        kernel = make_kernel(n_px, n_z, illum, rcv)
        V = pltpu.VMEM
        dma = pltpu.SemaphoreType.DMA
        regular = pltpu.SemaphoreType.REGULAR
        scratch = [
            V(cin.shape, BF16),
            V(rad.shape, BF16),
            V((2, dirs, units), BF16),
            V(far.shape, BF16),
            V(refl.shape, F32),
            V((2, 2, 3), F32),
            V(sd.shape, F32),
            V(rd.shape, F32),
            V(part.shape, jnp.int32),
            V(cnt.shape, jnp.int32),
            V(pw.shape, BF16),
            V((2 * LN, 2 * LN), BF16),
            V((2, TW, LN), F32),
            V((64, LN), F32),
            V((2, 32, LN), F32),
            V((2, 2, units), F32),
            V((2, 2, 3), F32),
            V((2, 8, dirs), F32),
            V((2, 8, rcv), F32),
            V((G, 64, units), BF16),
            V((128, units), BF16),
            V((2, G, 64, dirs), BF16),
            V((2, G, 2, 64, dirs), BF16),
            V((G, 64, dirs), F32),
            V((2, G, 2, 32, dirs), BF16),
            V((2, G, 2, 32, dirs), BF16),
            V((G, 64, units), BF16),
            V((2, TW, KC, LN), F32),
            V((128, units), BF16),
            V((LN, 2 * LN), BF16),
            V((G, n_px, 2 * qp, LN), BF16),
            V((G, n_px, 2 * qp, LN), BF16),
            V((G, 2 * qp, LN), BF16),
            V((n_z, 2 * qp, LN), BF16),
            dma((12,)),
            dma((2, 2)),
            dma((2, 2, 2)),
            dma((2, 2, G, 2)),
            dma((2, 2, G, 2)),
            dma((2, G)),
            dma((2,)),
            regular((max(1, len(doubling(n_z // 2))),)),
            regular((max(1, len(doubling(n_px - 1))),)),
        ]
        results = pl.pallas_call(
            kernel,
            out_shape=(
                pltpu.VMEM(cin.shape, BF16),
                pltpu.VMEM((kz, TW * qp), F32),
            ),
            in_specs=[pl.BlockSpec(memory_space=pltpu.HBM)] * 12,
            out_specs=(
                pl.BlockSpec(memory_space=pltpu.VMEM),
                pl.BlockSpec(memory_space=pltpu.VMEM),
            ),
            scratch_shapes=scratch,
            compiler_params=pltpu.CompilerParams(
                collective_id=0, has_side_effects=True, vmem_limit_bytes=60 << 20
            ),
        )(
            cin, rad, far, refl, jnp.transpose(cen, (1, 2, 0)), sd, rd, part, cnt, pw,
            jnp.asarray(second, BF16), jnp.asarray(twiddle),
        )
        return pl.pallas_call(
            hand_over,
            out_shape=(
                jax.ShapeDtypeStruct(cin.shape, BF16),
                jax.ShapeDtypeStruct((kz, TW * qp), F32),
            ),
            in_specs=[pl.BlockSpec(memory_space=pl.ANY)] * 2,
            out_specs=(pl.BlockSpec(memory_space=pl.ANY), pl.BlockSpec(memory_space=pl.ANY)),
            scratch_shapes=[dma((2,))],
            compiler_params=pltpu.CompilerParams(vmem_limit_bytes=1 << 20),
        )(*results)

    in_specs = (
        P("px", "py", None, None, None),
        P(),
        P(),
        P("px", "py", None),
        P(None, "px", "py"),
        P(),
        P(),
        P("px", "py", None),
        P("px", "py"),
        P("px", "py", None),
    )
    out_specs = (P("px", "py", None, None, None), P("py", "px"))
    return jax.shard_map(local, mesh=mesh, in_specs=in_specs, out_specs=out_specs, check_vma=False)
```
